32 devices in a mesh: scene: 4 (over x, core), view: 4 (over z), half: 2 (over y).
Axes of the slice: x: 2, y: 2, z: 4, core: 2. Of those that a mesh axis runs over, the one named last changes fastest.
Arguments:
- tokens: bfloat16 [16, 512, 2048], P(('scene', 'view'), 'half'), parts along dimension 0, may hold values from -9 to 12
- w_qkv: bfloat16 [2048, 768], replicated, may hold values from -0.125 to 0.125
- w_out: bfloat16 [256, 2048], replicated, may hold values from -5 to 5
- key_lists: int32 [16, 4, 2], P(('scene', 'view'), 'half'), parts along dimension 0, may hold values from 0 to 15, as said below
- list_len: int32 [16, 4], P(('scene', 'view'), 'half'), parts along dimension 0, may hold values from 1 to 2, as said below
Outputs:
- mixed: bfloat16 [16, 512, 2048], P(('scene', 'view'), 'half'), parts along dimension 0
The draws below stay inside these ranges and needn't reach their ends.
There are 4 independent parts, one for each index of `scene`. The reference program is written for one: setup_inputs(seed, part) draws one part's arguments, and reference() takes and returns one part's arrays. A program takes and returns all parts, laid end to end along the dimension named above; an argument that names none is the same for every part. Nothing has to cross between parts.
Inputs may be any that keep to these rules, and one draw needn't show every extreme that they name: `key_lists`: entries of one list are distinct block ids of the scene. `list_len`: some query block lists 2 blocks in every scene.
All inputs are finite; a program needn't handle non-finite values.
Results may differ from the reference program's by a relative error of at most 0.014.
The reference program's roundings to bfloat16 on the way (of `proj` and `attn`) count: a program that leaves them out, or rounds other values in their place, can miss the bound.
Values may be sent and summed in bfloat16 or wider, within the bound.
A program may use at most 64 MiB of HBM per device.

```python
import jax
import jax.numpy as jnp
from jax import lax

D = 2048
HEADS = 4
HD = 64
BLK = 128
TOKV = 512
VIEWS = 4
LMAX = 2


def draw_tokens(key, part):
    first = jax.random.fold_in(key, 0)
    shape = (VIEWS, TOKV, D)
    return jnp.clip(jax.random.normal(first, shape, jnp.float32), -6.0, 6.0).astype(jnp.bfloat16)


def draw_key_lists(key, part):
    blocks = VIEWS * TOKV // BLK
    raw = jax.random.randint(key, (blocks, blocks), 0, 65536)
    ranked = raw * blocks + jnp.arange(blocks, dtype=jnp.int32)[None, :]
    unused, picked = lax.top_k(ranked, LMAX)
    return picked.astype(jnp.int32).reshape(VIEWS, TOKV // BLK, LMAX)


def draw_list_len(key, part):
    blocks = VIEWS * TOKV // BLK
    lengths = jax.random.randint(key, (blocks,), 1, LMAX + 1)
    lengths = jnp.where(jnp.arange(blocks, dtype=jnp.int32) == 0, LMAX, lengths)
    return lengths.astype(jnp.int32).reshape(VIEWS, TOKV // BLK)


def gaussian(rng, shape, scale, most, held_as=jnp.bfloat16):
    array = scale * jax.random.normal(rng, shape, jnp.float32)
    return jnp.clip(array, min=-most, max=most).astype(held_as)


def setup_inputs(seed: int = 0, part: int = 0) -> dict:
    splits = jax.random.split(jax.random.key(seed), 6)
    own_keys = jax.random.split(jax.random.fold_in(splits[5], part), 6)
    return {
        "tokens": draw_tokens(jax.random.fold_in(jax.random.fold_in(splits[5], part), 71), part),
        "w_qkv": gaussian(splits[1], (D, 3 * HEADS * HD), D ** -0.5, 0.125),
        "w_out": gaussian(splits[2], (HEADS * HD, D), 1.0, 5.0),
        "key_lists": draw_key_lists(jax.random.fold_in(jax.random.fold_in(splits[5], part), 71), part),
        "list_len": draw_list_len(jax.random.fold_in(jax.random.fold_in(splits[5], part), 71), part),
    }


NEG = -1.0e30


def reference(tokens, w_qkv, w_out, key_lists, list_len):
    views, tokv, width = tokens.shape
    count = views * tokv
    flat = tokens.reshape(count, width)
    inner = w_out.shape[0]
    head_size = inner // HEADS
    proj = jnp.dot(flat, w_qkv, preferred_element_type=jnp.float32).astype(jnp.bfloat16)
    queries = proj[:, :inner]
    keys = proj[:, inner:2 * inner].reshape(count, HEADS, head_size).astype(jnp.float32)
    values = proj[:, 2 * inner:].reshape(count, HEADS, head_size).astype(jnp.float32)
    nblocks = count // BLK
    lists = key_lists.reshape(nblocks, -1)
    lengths = list_len.reshape(nblocks)
    slots = jnp.arange(lists.shape[1], dtype=jnp.int32)
    live = slots[None, :] < lengths[:, None]
    ids = jnp.arange(nblocks, dtype=jnp.int32)
    allowed = jnp.any((lists[:, :, None] == ids[None, None, :]) & live[:, :, None], axis=1)

    def one_block(item):
        block_q, mask = item
        keymask = jnp.repeat(mask, BLK)
        q3 = block_q.reshape(BLK, HEADS, head_size).astype(jnp.float32)
        scores = jnp.einsum("qhd,khd->hqk", q3, keys) * (head_size ** -0.5)
        masked = jnp.where(keymask[None, None, :], scores, NEG)
        top = jnp.max(masked, axis=2, keepdims=True)
        weights = jnp.where(keymask[None, None, :], jnp.exp(scores - top), 0.0)
        total = jnp.sum(weights, axis=2)
        rounded = lax.optimization_barrier(weights.astype(jnp.bfloat16)).astype(jnp.float32)
        summed = jnp.einsum("hqk,khd->qhd", rounded, values)
        return (summed / total.T[:, :, None]).reshape(BLK, inner).astype(jnp.bfloat16)

    attn = lax.map(one_block, (queries.reshape(nblocks, BLK, inner), allowed)).reshape(count, inner)
    mixed = jnp.dot(attn, w_out, preferred_element_type=jnp.float32).astype(jnp.bfloat16)
    return mixed.reshape(views, tokv, width)
```

```python
import functools

import jax
import jax.numpy as jnp
from jax import lax
from jax.experimental import pallas as pl
from jax.experimental.pallas import tpu as pltpu
from jax.sharding import PartitionSpec as P

HEADS = 4
NEG = -1e30
MESH = pl.DeviceIdType.MESH


def body(
    sizes,
    lists_hbm,
    lens_hbm,
    tokens_ref,
    w_ref,
    out_ref,
    x,
    w,
    kbuf,
    vbuf,
    weight_buf,
    total_buf,
    load_sem,
    send_sem,
    recv_sem,
    lists_ref,
    lens_ref,
    small_sem,
    xsem,
):
    views, halves = sizes
    view, half = lax.axis_index("view"), lax.axis_index("half")
    count, block, inner = kbuf.shape
    local = count // (views * halves)
    rows = local * block
    head_size = inner // HEADS
    slots = lists_ref.shape[1]
    small = [pltpu.make_async_copy(lists_hbm, lists_ref, small_sem.at[0]), pltpu.make_async_copy(lens_hbm, lens_ref, small_sem.at[1])]
    bufs = (kbuf, vbuf)

    loads = []
    for n, group in enumerate((1, 2, 0)):
        cols = pl.ds(group * inner, inner)
        loads.append(
            pltpu.make_async_copy(w_ref.at[:, cols], w.at[group], load_sem.at[n])
        )
    xl = [pltpu.make_async_copy(tokens_ref.at[pl.ds(b * block, block)], x.at[pl.ds(b * block, block)], xsem.at[b]) for b in range(local)]
    xl[0].start()
    loads[0].start()
    for l in xl[1:]:
        l.start()
    for l in loads[1:]:
        l.start()
    for cp in small:
        cp.start()

    toward = (
        (view + 1 < views, {"view": view + 1}, views),
        (view >= 1, {"view": view - 1}, views),
        (half + 1 < halves, {"half": half + 1}, halves),
        (half >= 1, {"half": half - 1}, halves),
    )

    barrier = pltpu.get_barrier_semaphore()
    for there, device, size in toward:
        if size > 1:

            @pl.when(there)
            def _():
                pl.semaphore_signal(barrier, inc=1, device_id=device, device_id_type=MESH)

    def piece(c, slot, way):
        rows_of = bufs[c].at[slot]
        return pltpu.make_async_remote_copy(
            src_ref=rows_of,
            dst_ref=rows_of,
            send_sem=send_sem.at[way, c, slot],
            recv_sem=recv_sem.at[c, slot],
            device_id=toward[way][1],
            device_id_type=MESH,
        )

    sends = []

    def send(c, slot, way, here):
        there, _, size = toward[way]
        if size == 1:
            return
        cond = there if here is None else jnp.logical_and(here, there)
        sends.append((cond, c, slot, way))

        @pl.when(cond)
        def _():
            piece(c, slot, way).start()

    def arrive(c, slot, here):
        @pl.when(here)
        def _():
            piece(c, slot, 0).wait_recv()

    def project(group):
        return jnp.dot(x[...], w[group], preferred_element_type=jnp.float32).astype(
            jnp.bfloat16
        )

    own = view * halves + half
    for c in range(2):
        loads[c].wait()
        for b in range(local):
            if c == 0:
                xl[b].wait()
            bufs[c][own * local + b] = jnp.dot(
                x[b * block : (b + 1) * block], w[1 + c], preferred_element_type=jnp.float32
            ).astype(jnp.bfloat16)
            if c == 0 and b == 0:
                expected = sum(there.astype(jnp.int32) for there, _, size in toward if size > 1)
                pl.semaphore_wait(barrier, expected)
            for way in (2, 3, 0, 1):
                send(c, own * local + b, way, None)

    loads[2].wait()
    for cp in small:
        cp.wait()
    queries = project(0)
    head_of = lax.broadcasted_iota(jnp.int32, (block, inner), 1) // head_size
    mine = [head_of == h for h in range(HEADS)]

    balanced = halves == 2 and views > 2
    last = views - 1

    def along_view(c, dist):
        for b in range(local):
            for sign, way in ((-1, 0), (1, 1)):
                shard = view + sign * dist
                here = shard >= 0 if sign < 0 else shard < views
                slot = (shard * halves + half) * local + b
                arrive(c, slot, here)
                across = here
                if balanced and c == 1:
                    across = shard >= 1 if sign < 0 else shard < last
                for out in (2, 3):
                    send(c, slot, out, across)
                if dist + 1 < views:
                    send(c, slot, way, here)

    def relay(dist):
        for b in range(local):
            for shard, here, way in ((0, view == dist, 0), (last, view == last - dist, 1)):
                slot = (shard * halves + (halves - 1) - half) * local + b
                arrive(1, slot, here)
                if dist < last:
                    send(1, slot, way, here)

    def along_half(c):
        for far in range(1, halves):
            for dist in range(views):
                for b in range(local):
                    for sign in (-1, 1) if dist else (1,):
                        shard = view + sign * dist
                        seen = shard >= 0 if sign < 0 else shard < views
                        if balanced and c == 1:
                            seen = jnp.logical_and(shard >= 1, shard < last)
                        for side, way in ((-1, 2), (1, 3)):
                            other = half + side * far
                            here = jnp.logical_and(
                                seen, other >= 0 if side < 0 else other < halves
                            )
                            slot = (shard * halves + other) * local + b
                            arrive(c, slot, here)
                            if far + 1 < halves:
                                send(c, slot, way, here)

    for dist in range(1, views):
        along_view(0, dist)
        if balanced and dist > 1:
            relay(dist - 1)
        along_view(1, dist)
        if balanced and dist == 1:
            relay(0)

    along_half(0)
    for i in range(local):
        q = queries[i * block : (i + 1) * block]
        stacked = jnp.concatenate([jnp.where(m, q, jnp.zeros_like(q)) for m in mine], axis=0)
        keys = jnp.concatenate([kbuf[lists_ref[i, s]] for s in range(slots)], axis=0)
        scores = lax.dot_general(
            stacked, keys, (((1,), (1,)), ((), ())), preferred_element_type=jnp.float32
        ) * head_size ** (-0.5)
        live = lax.broadcasted_iota(jnp.int32, scores.shape, 1) // block < lens_ref[i]
        top = jnp.max(jnp.where(live, scores, NEG), axis=1, keepdims=True)
        weights = jnp.where(live, jnp.exp(scores - top), 0.0)
        total_buf[i] = jnp.sum(weights, axis=1, keepdims=True)
        weight_buf[i] = weights.astype(jnp.bfloat16)

    along_half(1)
    if balanced:
        relay(last)
    for i in range(local):
        values = jnp.concatenate([vbuf[lists_ref[i, s]] for s in range(slots)], axis=0)
        summed = jnp.dot(weight_buf[i], values, preferred_element_type=jnp.float32)
        scaled = summed / total_buf[i]
        attn = jnp.zeros((block, inner), jnp.float32)
        for h, m in enumerate(mine):
            attn = jnp.where(m, scaled[h * block : (h + 1) * block], attn)
        out_ref[i * block : (i + 1) * block] = attn.astype(out_ref.dtype)

    for cond, c, slot, way in sends:

        @pl.when(cond)
        def _():
            piece(c, slot, way).wait_send()


def per_device(sizes, tokens, w_qkv, w_out, key_lists, list_len):
    views, halves = sizes
    rows, width = tokens.shape[1:]
    inner = w_out.shape[0]
    local = key_lists.shape[1]
    slots = key_lists.shape[2]
    block = rows // local
    shards = views * halves
    anywhere = pl.BlockSpec(memory_space=pltpu.HBM)
    attn = pl.pallas_call(
        functools.partial(body, sizes),
        out_shape=pltpu.VMEM((rows, inner), jnp.bfloat16),
        in_specs=[
            anywhere,
            anywhere,
            anywhere,
            anywhere,
        ],
        out_specs=pl.BlockSpec(memory_space=pltpu.VMEM),
        scratch_shapes=[
            pltpu.VMEM((rows, width), jnp.bfloat16),
            pltpu.VMEM((3, width, inner), jnp.bfloat16),
            pltpu.VMEM((shards * local, block, inner), jnp.bfloat16),
            pltpu.VMEM((shards * local, block, inner), jnp.bfloat16),
            pltpu.VMEM((local, HEADS * block, slots * block), jnp.bfloat16),
            pltpu.VMEM((local, HEADS * block, 1), jnp.float32),
            pltpu.SemaphoreType.DMA((4,)),
            pltpu.SemaphoreType.DMA((4, 2, shards * local)),
            pltpu.SemaphoreType.DMA((2, shards * local)),
            pltpu.SMEM((local, slots), jnp.int32),
            pltpu.SMEM((local,), jnp.int32),
            pltpu.SemaphoreType.DMA((2,)),
            pltpu.SemaphoreType.DMA((local,)),
        ],
        compiler_params=pltpu.CompilerParams(collective_id=0, has_side_effects=True, vmem_limit_bytes=62000000),
    )(
        key_lists.reshape(local, slots),
        list_len.reshape(local),
        tokens.reshape(rows, width),
        w_qkv,
    )
    mixed = jnp.dot(attn, w_out, preferred_element_type=jnp.float32).astype(jnp.bfloat16)
    return mixed.reshape(1, rows, width)


def solution(mesh):
    sizes = (mesh.shape["view"], mesh.shape["half"])
    placed = (
        P(("scene", "view"), "half", None),
        P(),
        P(),
        P(("scene", "view"), "half", None),
        P(("scene", "view"), "half"),
    )
    return jax.shard_map(
        functools.partial(per_device, sizes),
        mesh=mesh,
        in_specs=placed,
        out_specs=P(("scene", "view"), "half", None),
        check_vma=False,
    )
```

```python
import functools

import jax
import jax.numpy as jnp
from jax import lax
from jax.experimental import pallas as pl
from jax.experimental.pallas import tpu as pltpu
from jax.sharding import PartitionSpec as P

HEADS = 4
NEG = -1e30
MESH = pl.DeviceIdType.MESH


def body(
    sizes,
    lists_hbm,
    lens_hbm,
    tokens_ref,
    w_ref,
    out_ref,
    x,
    w,
    kbuf,
    vbuf,
    weight_buf,
    total_buf,
    load_sem,
    send_sem,
    recv_sem,
    lists_ref,
    lens_ref,
    small_sem,
    xsem,
):
    views, halves = sizes
    view, half = lax.axis_index("view"), lax.axis_index("half")
    count, block, inner = kbuf.shape
    local = count // (views * halves)
    rows = local * block
    head_size = inner // HEADS
    slots = lists_ref.shape[1]
    small = [pltpu.make_async_copy(lists_hbm, lists_ref, small_sem.at[0]), pltpu.make_async_copy(lens_hbm, lens_ref, small_sem.at[1])]
    bufs = (kbuf, vbuf)

    loads = []
    for n, group in enumerate((1, 2, 0)):
        cols = pl.ds(group * inner, inner)
        loads.append(
            pltpu.make_async_copy(w_ref.at[:, cols], w.at[group], load_sem.at[n])
        )
    xl = [pltpu.make_async_copy(tokens_ref.at[pl.ds(b * block, block)], x.at[pl.ds(b * block, block)], xsem.at[b]) for b in range(local)]
    xl[0].start()
    loads[0].start()
    for l in xl[1:]:
        l.start()
    for l in loads[1:]:
        l.start()
    for cp in small:
        cp.start()

    toward = (
        (view + 1 < views, {"view": view + 1}, views),
        (view >= 1, {"view": view - 1}, views),
        (half + 1 < halves, {"half": half + 1}, halves),
        (half >= 1, {"half": half - 1}, halves),
    )

    barrier = pltpu.get_barrier_semaphore()
    for there, device, size in toward:
        if size > 1:

            @pl.when(there)
            def _():
                pl.semaphore_signal(barrier, inc=1, device_id=device, device_id_type=MESH)

    def piece(c, slot, way):
        rows_of = bufs[c].at[slot]
        return pltpu.make_async_remote_copy(
            src_ref=rows_of,
            dst_ref=rows_of,
            send_sem=send_sem.at[way, c, slot],
            recv_sem=recv_sem.at[c, slot],
            device_id=toward[way][1],
            device_id_type=MESH,
        )

    sends = []

    def send(c, slot, way, here):
        there, _, size = toward[way]
        if size == 1:
            return
        cond = there if here is None else jnp.logical_and(here, there)
        sends.append((cond, c, slot, way))

        @pl.when(cond)
        def _():
            piece(c, slot, way).start()

    def arrive(c, slot, here):
        @pl.when(here)
        def _():
            piece(c, slot, 0).wait_recv()

    def project(group):
        return jnp.dot(x[...], w[group], preferred_element_type=jnp.float32).astype(
            jnp.bfloat16
        )

    own = view * halves + half
    for c in range(2):
        loads[c].wait()
        for b in range(local):
            if c == 0:
                xl[b].wait()
            bufs[c][own * local + b] = jnp.dot(
                x[b * block : (b + 1) * block], w[1 + c], preferred_element_type=jnp.float32
            ).astype(jnp.bfloat16)
            if c == 0 and b == 0:
                expected = sum(there.astype(jnp.int32) for there, _, size in toward if size > 1)
                pl.semaphore_wait(barrier, expected)
            for way in (2, 3, 0, 1):
                send(c, own * local + b, way, None)

    loads[2].wait()
    for cp in small:
        cp.wait()
    queries = project(0)
    head_of = lax.broadcasted_iota(jnp.int32, (block, inner), 1) // head_size
    mine = [head_of == h for h in range(HEADS)]

    balanced = halves == 2 and views > 2
    last = views - 1

    def along_view(c, dist):
        for b in range(local):
            for sign, way in ((-1, 0), (1, 1)):
                shard = view + sign * dist
                here = shard >= 0 if sign < 0 else shard < views
                slot = (shard * halves + half) * local + b
                arrive(c, slot, here)
                across = here
                if balanced and c == 1:
                    across = shard >= 1 if sign < 0 else shard < last
                for out in (2, 3):
                    send(c, slot, out, across)
                if dist + 1 < views:
                    send(c, slot, way, here)

    def relay(dist):
        for b in range(local):
            for shard, here, way in ((0, view == dist, 0), (last, view == last - dist, 1)):
                slot = (shard * halves + (halves - 1) - half) * local + b
                arrive(1, slot, here)
                if dist < last:
                    send(1, slot, way, here)

    def along_half(c):
        for far in range(1, halves):
            for dist in range(views):
                for b in range(local):
                    for sign in (-1, 1) if dist else (1,):
                        shard = view + sign * dist
                        seen = shard >= 0 if sign < 0 else shard < views
                        if balanced and c == 1:
                            seen = jnp.logical_and(shard >= 1, shard < last)
                        for side, way in ((-1, 2), (1, 3)):
                            other = half + side * far
                            here = jnp.logical_and(
                                seen, other >= 0 if side < 0 else other < halves
                            )
                            slot = (shard * halves + other) * local + b
                            arrive(c, slot, here)
                            if far + 1 < halves:
                                send(c, slot, way, here)

    for dist in range(1, views):
        along_view(0, dist)
        if balanced and dist > 1:
            relay(dist - 1)
        along_view(1, dist)
        if balanced and dist == 1:
            relay(0)

    along_half(0)
    for i in range(local):
        q = queries[i * block : (i + 1) * block]
        stacked = jnp.concatenate([jnp.where(m, q, jnp.zeros_like(q)) for m in mine], axis=0)
        keys = jnp.concatenate([kbuf[lists_ref[i, s]] for s in range(slots)], axis=0)
        scores = lax.dot_general(
            stacked, keys, (((1,), (1,)), ((), ())), preferred_element_type=jnp.float32
        ) * head_size ** (-0.5)
        live = lax.broadcasted_iota(jnp.int32, scores.shape, 1) // block < lens_ref[i]
        top = jnp.max(jnp.where(live, scores, NEG), axis=1, keepdims=True)
        weights = jnp.where(live, jnp.exp(scores - top), 0.0)
        total_buf[i] = jnp.sum(weights, axis=1, keepdims=True)
        weight_buf[i] = weights.astype(jnp.bfloat16)

    along_half(1)
    if balanced:
        relay(last)
    for i in range(local):
        values = jnp.concatenate([vbuf[lists_ref[i, s]] for s in range(slots)], axis=0)
        summed = jnp.dot(weight_buf[i], values, preferred_element_type=jnp.float32)
        scaled = summed / total_buf[i]
        attn = jnp.zeros((block, inner), jnp.float32)
        for h, m in enumerate(mine):
            attn = jnp.where(m, scaled[h * block : (h + 1) * block], attn)
        out_ref[i * block : (i + 1) * block] = attn.astype(out_ref.dtype)

    for cond, c, slot, way in sends:

        @pl.when(cond)
        def _():
            piece(c, slot, way).wait_send()


def listed(entries, block):
    hit = entries[0] == block
    for entry in entries[1:]:
        hit = jnp.logical_or(hit, entry == block)
    return hit.astype(jnp.int32)


def places(flags, count):
    slots, after = [], 0
    for flag in reversed(flags):
        slots.append(jnp.where(flag == 1, count - 1 - after, -1))
        after = after + flag
    return slots[::-1]


def chosen(slots, values, slot, empty):
    out = empty
    for s, value in zip(slots, values):
        out = jnp.where(s == slot, value, out)
    return out


def paired_body(
    sizes,
    lists_hbm,
    lens_hbm,
    tokens_ref,
    w_ref,
    out_ref,
    x,
    w,
    kbuf,
    vbuf,
    zstage,
    ystage,
    weight_buf,
    total_buf,
    x_sem,
    w_sem,
    small_sem,
    send_sem,
    recv_sem,
    list_send_sem,
    list_recv_sem,
    *small,
):
    views, halves = sizes
    view, half = lax.axis_index("view"), lax.axis_index("half")
    block, inner = kbuf.shape[1:]
    local = x.shape[0] // block
    head_size = inner // HEADS
    lists, lens = small[:4], small[4:]
    slots = lists[0].shape[1]
    bufs = (kbuf, vbuf)
    quota = local * slots

    loads = [
        pltpu.make_async_copy(
            tokens_ref.at[pl.ds(b * block, block)], x.at[pl.ds(b * block, block)], x_sem.at[b]
        )
        for b in range(local)
    ]
    w_loads = [
        pltpu.make_async_copy(w_ref.at[:, pl.ds(group * inner, inner)], w.at[group], w_sem.at[n])
        for n, group in enumerate((1, 2, 0))
    ]
    own_lists = [
        pltpu.make_async_copy(lists_hbm, lists[0], small_sem.at[0]),
        pltpu.make_async_copy(lens_hbm, lens[0], small_sem.at[1]),
    ]
    for load in (loads[0], w_loads[0], *loads[1:], *w_loads[1:], *own_lists):
        load.start()

    left = view < views // 2
    end_view = jnp.where(left, 0, views - 1)
    inner_view = jnp.where(left, 1, views - 2)
    cross_view = views - 1 - inner_view
    far_view = views - 1 - end_view
    at_end = view == end_view
    mate_view = jnp.where(at_end, inner_view, end_view)
    other = halves - 1 - half
    mate = {"view": mate_view}
    beside = {"half": other}
    diagonal = {"view": mate_view, "half": other}
    cross = {"view": cross_view}

    barrier = pltpu.get_barrier_semaphore()
    for device in (mate, beside, diagonal):
        pl.semaphore_signal(barrier, inc=1, device_id=device, device_id_type=MESH)

    @pl.when(jnp.logical_not(at_end))
    def _():
        pl.semaphore_signal(barrier, inc=1, device_id=cross, device_id_type=MESH)

    links = (mate, beside, cross)

    def copy(c, link, n, src, to):
        return pltpu.make_async_remote_copy(
            src_ref=src,
            dst_ref=bufs[c].at[to],
            send_sem=send_sem.at[c, link, n],
            recv_sem=recv_sem.at[c, to],
            device_id=links[link],
            device_id_type=MESH,
        )

    def arrived(c, *slots_of):
        for to in slots_of:
            copy(c, 0, 0, bufs[c].at[to], to).wait_recv()

    def list_copies(to, device, n):
        return [
            pltpu.make_async_remote_copy(
                src_ref=src,
                dst_ref=dst,
                send_sem=list_send_sem.at[n, k],
                recv_sem=list_recv_sem.at[to, k],
                device_id=device,
                device_id_type=MESH,
            )
            for k, (src, dst) in enumerate(((lists_hbm, lists[to]), (lens_hbm, lens[to])))
        ]

    list_routes = ((1, beside), (2, mate), (3, diagonal))

    def project(c, b):
        bufs[c][b] = jnp.dot(
            x[b * block : (b + 1) * block], w[1 + c], preferred_element_type=jnp.float32
        ).astype(jnp.bfloat16)

    last = local - 1
    z_first, z_rest = local, local + 1
    z_count = quota
    over = 4 * local
    picks_inner, picks_end = over + 1, z_rest + z_count

    def own_sends(c, b):
        @pl.when(at_end)
        def _():
            copy(c, 0, b, bufs[c].at[b], local + b).start()

        @pl.when(jnp.logical_not(at_end))
        def _():
            copy(c, 2, b, bufs[c].at[b], 2 * local + b).start()
            if b == 0:
                copy(c, 0, 0, bufs[c].at[0], z_first).start()
            if b == last:
                copy(c, 1, 0, bufs[c].at[last], over).start()

    for c in range(2):
        w_loads[c].wait()
        for b in range(local):
            if c == 0:
                loads[b].wait()
            project(c, b)
            if c == 0 and b == 0:
                pl.semaphore_wait(barrier, jnp.where(at_end, 3, 4))
                for n, (to, device) in enumerate(list_routes):
                    for send in list_copies(to, device, n):
                        send.start()
            own_sends(c, b)

    w_loads[2].wait()
    queries = jnp.dot(x[...], w[0], preferred_element_type=jnp.float32).astype(jnp.bfloat16)
    for load in own_lists:
        load.wait()
    for n, (to, device) in enumerate(list_routes):
        for send in list_copies(to, device, n):
            send.wait_recv()

    def entries(k):
        return [
            jnp.where(s < lens[k][i], lists[k][i, s], -1) for i in range(local) for s in range(slots)
        ]

    def ids(of_view, of_half):
        return [(of_view * halves + of_half) * local + b for b in range(local)]

    mine, theirs = entries(0), entries(1)

    def passed(ends):
        inners, crosses, fars = (
            [ids(v, h) for h in (half, other)] for v in (inner_view, cross_view, far_view)
        )
        needs, totals = [], []
        for r in range(2):
            needs.append([listed(ends, i) for i in (inners[r][last], *crosses[r], *fars[r])])
            totals.append(sum(needs[r]))
        out = []
        for r in range(2):
            spill = (totals[r] > z_count).astype(jnp.int32)
            take = (totals[1 - r] > z_count).astype(jnp.int32)
            flags = [needs[r][0] * (1 - spill), take, *needs[r][1:]]
            names = [inners[r][last], inners[1 - r][last], *crosses[r], *fars[r]]
            out.append((names, places(flags, z_count)))
        return out

    def positions(names, slots_of, first):
        out = []
        for entry in mine:
            at = 0
            for name, slot in zip(names, slots_of):
                at = jnp.where(jnp.logical_and(entry == name, slot >= 0), first + slot, at)
            out.append(at)
        return out

    def merge(*tables):
        return [functools.reduce(jnp.maximum, column) for column in zip(*tables)]

    def stage(c, stage_buf, k, slots_of, sources, count):
        reach = k + len(sources) - count + 1
        value = bufs[c][sources[0]]
        for j in range(1, reach):
            value = jnp.where(slots_of[j] == k, bufs[c][sources[j]], value)
        stage_buf[c, k] = value

    head_of = lax.broadcasted_iota(jnp.int32, (block, inner), 1) // head_size
    heads = [head_of == h for h in range(HEADS)]

    def weigh(at):
        for i in range(local):
            q = queries[i * block : (i + 1) * block]
            stacked = jnp.concatenate([jnp.where(m, q, jnp.zeros_like(q)) for m in heads], axis=0)
            keys = jnp.concatenate([kbuf[at[i * slots + s]] for s in range(slots)], axis=0)
            scores = lax.dot_general(
                stacked, keys, (((1,), (1,)), ((), ())), preferred_element_type=jnp.float32
            ) * head_size ** (-0.5)
            live = lax.broadcasted_iota(jnp.int32, scores.shape, 1) // block < lens[0][i]
            top = jnp.max(jnp.where(live, scores, NEG), axis=1, keepdims=True)
            weights = jnp.where(live, jnp.exp(scores - top), 0.0)
            total_buf[i] = jnp.sum(weights, axis=1, keepdims=True)
            weight_buf[i] = weights.astype(jnp.bfloat16)

    def finish(at):
        for i in range(local):
            values = jnp.concatenate([vbuf[at[i * slots + s]] for s in range(slots)], axis=0)
            summed = jnp.dot(weight_buf[i], values, preferred_element_type=jnp.float32)
            scaled = summed / total_buf[i]
            attn = jnp.zeros((block, inner), jnp.float32)
            for h, m in enumerate(heads):
                attn = jnp.where(m, scaled[h * block : (h + 1) * block], attn)
            out_ref[i * block : (i + 1) * block] = attn.astype(out_ref.dtype)

    def sent(c, link, n):
        copy(c, link, n, bufs[c].at[0], 0).wait_send()

    @pl.when(jnp.logical_not(at_end))
    def _():
        own, ends, crosses, fars = (
            [g * local + b for b in range(local)] for g in range(4)
        )
        z_slots = passed(entries(2) + entries(3))[0][1]
        z_sources = [own[last], over, *crosses, *fars]
        groups = (inner_view, end_view, cross_view, far_view)

        def order(table):
            o, e, k, f = table
            mixed = [v for pair in zip(e, k) for v in pair]
            return [*o[:last], e[0], k[0], *mixed[2:], *f]

        y_sources = order((own, ends, crosses, fars))

        def picks(listing, of_half):
            names = order([ids(v, of_half) for v in groups])
            return names, places([listed(listing, name) for name in names], quota)

        y_slots = picks(theirs, half)[1]
        in_names, in_slots = picks(mine, other)
        row = [i for v in groups for i in ids(v, half)]
        at = merge(
            positions(row, [jnp.int32(j) for j in range(len(row))], 0),
            positions([ids(inner_view, other)[last]], [jnp.int32(0)], over),
            positions(in_names, in_slots, picks_inner),
        )

        def z(c, k):
            stage(c, zstage, k, z_slots, z_sources, z_count)
            copy(c, 0, 1 + k, zstage.at[c, k], z_rest + k).start()

        def y(c, k):
            stage(c, ystage, k, y_slots, y_sources, quota)
            copy(c, 1, 1 + k, ystage.at[c, k], picks_inner + k).start()

        for c in range(2):
            for b in range(local):
                arrived(c, ends[b])
                copy(c, 2, local + b, bufs[c].at[ends[b]], 3 * local + b).start()
                arrived(c, crosses[b])
                if b == 0:
                    arrived(c, over)
                z(c, b)
                if b == last:
                    for k in range(local):
                        y(c, k)
        for c in range(2):
            for b in range(local):
                arrived(c, fars[b])
                z(c, local + b)
                y(c, local + b)
        arrived(0, *range(picks_inner, picks_inner + quota))
        weigh(at)
        arrived(1, *range(picks_inner, picks_inner + quota))
        finish(at)
        for c in range(2):
            for n in range(2 * local):
                sent(c, 2, n)
            for n in range(1 + z_count):
                sent(c, 0, n)
            for n in range(1 + quota):
                sent(c, 1, n)

    @pl.when(at_end)
    def _():
        here, there = passed(mine + theirs)
        sources = [*range(local), z_first, *range(z_rest, z_rest + z_count)]

        def held(table, of_half):
            names, slots_of = table
            return [
                *ids(end_view, of_half),
                ids(inner_view, of_half)[0],
                *(chosen(slots_of, names, k, jnp.int32(-2)) for k in range(z_count)),
            ]

        own_names, in_names = held(here, half), held(there, other)
        y_slots = places([listed(theirs, name) for name in own_names], quota)
        in_slots = places([listed(mine, name) for name in in_names], quota)
        at = merge(
            positions(own_names, [jnp.int32(j) for j in range(len(own_names))], 0),
            positions(in_names, in_slots, picks_end),
        )

        def y(c, k):
            stage(c, ystage, k, y_slots, sources, quota)
            copy(c, 1, k, ystage.at[c, k], picks_end + k).start()

        for part in range(2):
            for c in range(2):
                if part == 0:
                    arrived(c, z_first)
                for k in range(part * local, (part + 1) * local):
                    arrived(c, z_rest + k)
                    y(c, k)
        arrived(0, *range(picks_end, picks_end + quota))
        weigh(at)
        arrived(1, *range(picks_end, picks_end + quota))
        finish(at)
        for c in range(2):
            for n in range(local):
                sent(c, 0, n)
            for n in range(quota):
                sent(c, 1, n)

    for n, (to, device) in enumerate(list_routes):
        for send in list_copies(to, device, n):
            send.wait_send()


def paired(sizes, block, tokens, w_qkv, lists, lens, inner):
    rows, width = tokens.shape
    local, slots = lists.shape
    quota = local * slots
    count = 4 * local + 1 + quota
    anywhere = pl.BlockSpec(memory_space=pl.ANY)
    return pl.pallas_call(
        functools.partial(paired_body, sizes),
        out_shape=pltpu.VMEM((rows, inner), jnp.bfloat16),
        in_specs=[anywhere] * 4,
        out_specs=pl.BlockSpec(memory_space=pltpu.VMEM),
        scratch_shapes=[
            pltpu.VMEM((rows, width), jnp.bfloat16),
            pltpu.VMEM((3, width, inner), jnp.bfloat16),
            pltpu.VMEM((count, block, inner), jnp.bfloat16),
            pltpu.VMEM((count, block, inner), jnp.bfloat16),
            pltpu.VMEM((2, quota, block, inner), jnp.bfloat16),
            pltpu.VMEM((2, quota, block, inner), jnp.bfloat16),
            pltpu.VMEM((local, HEADS * block, slots * block), jnp.bfloat16),
            pltpu.VMEM((local, HEADS * block, 1), jnp.float32),
            pltpu.SemaphoreType.DMA((local,)),
            pltpu.SemaphoreType.DMA((3,)),
            pltpu.SemaphoreType.DMA((2,)),
            pltpu.SemaphoreType.DMA((2, 3, max(2 * local, 1 + quota))),
            pltpu.SemaphoreType.DMA((2, count)),
            pltpu.SemaphoreType.DMA((3, 2)),
            pltpu.SemaphoreType.DMA((4, 2)),
            *[pltpu.SMEM((local, slots), jnp.int32)] * 4,
            *[pltpu.SMEM((local,), jnp.int32)] * 4,
        ],
        compiler_params=pltpu.CompilerParams(
            collective_id=0, has_side_effects=True, vmem_limit_bytes=62000000
        ),
    )(lists, lens, tokens, w_qkv)


def project_out(attn, w_out):
    mixed = jnp.dot(attn, w_out, preferred_element_type=jnp.float32).astype(jnp.bfloat16)
    return mixed.reshape(1, *mixed.shape)


def per_device(sizes, tokens, w_qkv, w_out, key_lists, list_len):
    views, halves = sizes
    rows, width = tokens.shape[1:]
    inner = w_out.shape[0]
    local = key_lists.shape[1]
    slots = key_lists.shape[2]
    block = rows // local
    shards = views * halves
    if views == 4 and halves == 2 and local == 2 and slots == 2:
        attn = paired(
            sizes,
            block,
            tokens.reshape(rows, width),
            w_qkv,
            key_lists.reshape(local, slots),
            list_len.reshape(local),
            inner,
        )
        return project_out(attn, w_out)
    anywhere = pl.BlockSpec(memory_space=pl.ANY)
    attn = pl.pallas_call(
        functools.partial(body, sizes),
        out_shape=pltpu.VMEM((rows, inner), jnp.bfloat16),
        in_specs=[
            anywhere,
            anywhere,
            anywhere,
            anywhere,
        ],
        out_specs=pl.BlockSpec(memory_space=pltpu.VMEM),
        scratch_shapes=[
            pltpu.VMEM((rows, width), jnp.bfloat16),
            pltpu.VMEM((3, width, inner), jnp.bfloat16),
            pltpu.VMEM((shards * local, block, inner), jnp.bfloat16),
            pltpu.VMEM((shards * local, block, inner), jnp.bfloat16),
            pltpu.VMEM((local, HEADS * block, slots * block), jnp.bfloat16),
            pltpu.VMEM((local, HEADS * block, 1), jnp.float32),
            pltpu.SemaphoreType.DMA((4,)),
            pltpu.SemaphoreType.DMA((4, 2, shards * local)),
            pltpu.SemaphoreType.DMA((2, shards * local)),
            pltpu.SMEM((local, slots), jnp.int32),
            pltpu.SMEM((local,), jnp.int32),
            pltpu.SemaphoreType.DMA((2,)),
            pltpu.SemaphoreType.DMA((local,)),
        ],
        compiler_params=pltpu.CompilerParams(collective_id=0, has_side_effects=True, vmem_limit_bytes=62000000),
    )(
        key_lists.reshape(local, slots),
        list_len.reshape(local),
        tokens.reshape(rows, width),
        w_qkv,
    )
    return project_out(attn, w_out)


def solution(mesh):
    sizes = (mesh.shape["view"], mesh.shape["half"])
    placed = (
        P(("scene", "view"), "half", None),
        P(),
        P(),
        P(("scene", "view"), "half", None),
        P(("scene", "view"), "half"),
    )
    return jax.shard_map(
        functools.partial(per_device, sizes),
        mesh=mesh,
        in_specs=placed,
        out_specs=P(("scene", "view"), "half", None),
        check_vma=False,
    )
```

```python
import functools

import jax
import jax.numpy as jnp
from jax import lax
from jax.experimental import pallas as pl
from jax.experimental.pallas import tpu as pltpu
from jax.sharding import PartitionSpec as P

HEADS = 4
NEG = -1e30
MESH = pl.DeviceIdType.MESH


def body(
    sizes,
    lists_hbm,
    lens_hbm,
    tokens_ref,
    w_ref,
    out_ref,
    x,
    w,
    kbuf,
    vbuf,
    weight_buf,
    total_buf,
    load_sem,
    send_sem,
    recv_sem,
    lists_ref,
    lens_ref,
    small_sem,
    xsem,
):
    views, halves = sizes
    view, half = lax.axis_index("view"), lax.axis_index("half")
    count, block, inner = kbuf.shape
    local = count // (views * halves)
    rows = local * block
    head_size = inner // HEADS
    slots = lists_ref.shape[1]
    small = [pltpu.make_async_copy(lists_hbm, lists_ref, small_sem.at[0]), pltpu.make_async_copy(lens_hbm, lens_ref, small_sem.at[1])]
    bufs = (kbuf, vbuf)

    loads = []
    for n, group in enumerate((1, 2, 0)):
        cols = pl.ds(group * inner, inner)
        loads.append(
            pltpu.make_async_copy(w_ref.at[:, cols], w.at[group], load_sem.at[n])
        )
    xl = [pltpu.make_async_copy(tokens_ref.at[pl.ds(b * block, block)], x.at[pl.ds(b * block, block)], xsem.at[b]) for b in range(local)]
    xl[0].start()
    loads[0].start()
    for l in xl[1:]:
        l.start()
    for l in loads[1:]:
        l.start()
    for cp in small:
        cp.start()

    toward = (
        (view + 1 < views, {"view": view + 1}, views),
        (view >= 1, {"view": view - 1}, views),
        (half + 1 < halves, {"half": half + 1}, halves),
        (half >= 1, {"half": half - 1}, halves),
    )

    barrier = pltpu.get_barrier_semaphore()
    for there, device, size in toward:
        if size > 1:

            @pl.when(there)
            def _():
                pl.semaphore_signal(barrier, inc=1, device_id=device, device_id_type=MESH)

    def piece(c, slot, way):
        rows_of = bufs[c].at[slot]
        return pltpu.make_async_remote_copy(
            src_ref=rows_of,
            dst_ref=rows_of,
            send_sem=send_sem.at[way, c, slot],
            recv_sem=recv_sem.at[c, slot],
            device_id=toward[way][1],
            device_id_type=MESH,
        )

    sends = []

    def send(c, slot, way, here):
        there, _, size = toward[way]
        if size == 1:
            return
        cond = there if here is None else jnp.logical_and(here, there)
        sends.append((cond, c, slot, way))

        @pl.when(cond)
        def _():
            piece(c, slot, way).start()

    def arrive(c, slot, here):
        @pl.when(here)
        def _():
            piece(c, slot, 0).wait_recv()

    def project(group):
        return jnp.dot(x[...], w[group], preferred_element_type=jnp.float32).astype(
            jnp.bfloat16
        )

    own = view * halves + half
    for c in range(2):
        loads[c].wait()
        for b in range(local):
            if c == 0:
                xl[b].wait()
            bufs[c][own * local + b] = jnp.dot(
                x[b * block : (b + 1) * block], w[1 + c], preferred_element_type=jnp.float32
            ).astype(jnp.bfloat16)
            if c == 0 and b == 0:
                expected = sum(there.astype(jnp.int32) for there, _, size in toward if size > 1)
                pl.semaphore_wait(barrier, expected)
            for way in (2, 3, 0, 1):
                send(c, own * local + b, way, None)

    loads[2].wait()
    for cp in small:
        cp.wait()
    queries = project(0)
    head_of = lax.broadcasted_iota(jnp.int32, (block, inner), 1) // head_size
    mine = [head_of == h for h in range(HEADS)]

    balanced = halves == 2 and views > 2
    last = views - 1

    def along_view(c, dist):
        for b in range(local):
            for sign, way in ((-1, 0), (1, 1)):
                shard = view + sign * dist
                here = shard >= 0 if sign < 0 else shard < views
                slot = (shard * halves + half) * local + b
                arrive(c, slot, here)
                across = here
                if balanced and c == 1:
                    across = shard >= 1 if sign < 0 else shard < last
                for out in (2, 3):
                    send(c, slot, out, across)
                if dist + 1 < views:
                    send(c, slot, way, here)

    def relay(dist):
        for b in range(local):
            for shard, here, way in ((0, view == dist, 0), (last, view == last - dist, 1)):
                slot = (shard * halves + (halves - 1) - half) * local + b
                arrive(1, slot, here)
                if dist < last:
                    send(1, slot, way, here)

    def along_half(c):
        for far in range(1, halves):
            for dist in range(views):
                for b in range(local):
                    for sign in (-1, 1) if dist else (1,):
                        shard = view + sign * dist
                        seen = shard >= 0 if sign < 0 else shard < views
                        if balanced and c == 1:
                            seen = jnp.logical_and(shard >= 1, shard < last)
                        for side, way in ((-1, 2), (1, 3)):
                            other = half + side * far
                            here = jnp.logical_and(
                                seen, other >= 0 if side < 0 else other < halves
                            )
                            slot = (shard * halves + other) * local + b
                            arrive(c, slot, here)
                            if far + 1 < halves:
                                send(c, slot, way, here)

    for dist in range(1, views):
        along_view(0, dist)
        if balanced and dist > 1:
            relay(dist - 1)
        along_view(1, dist)
        if balanced and dist == 1:
            relay(0)

    along_half(0)
    for i in range(local):
        q = queries[i * block : (i + 1) * block]
        stacked = jnp.concatenate([jnp.where(m, q, jnp.zeros_like(q)) for m in mine], axis=0)
        keys = jnp.concatenate([kbuf[lists_ref[i, s]] for s in range(slots)], axis=0)
        scores = lax.dot_general(
            stacked, keys, (((1,), (1,)), ((), ())), preferred_element_type=jnp.float32
        ) * head_size ** (-0.5)
        live = lax.broadcasted_iota(jnp.int32, scores.shape, 1) // block < lens_ref[i]
        top = jnp.max(jnp.where(live, scores, NEG), axis=1, keepdims=True)
        weights = jnp.where(live, jnp.exp(scores - top), 0.0)
        total_buf[i] = jnp.sum(weights, axis=1, keepdims=True)
        weight_buf[i] = weights.astype(jnp.bfloat16)

    along_half(1)
    if balanced:
        relay(last)
    for i in range(local):
        values = jnp.concatenate([vbuf[lists_ref[i, s]] for s in range(slots)], axis=0)
        summed = jnp.dot(weight_buf[i], values, preferred_element_type=jnp.float32)
        scaled = summed / total_buf[i]
        attn = jnp.zeros((block, inner), jnp.float32)
        for h, m in enumerate(mine):
            attn = jnp.where(m, scaled[h * block : (h + 1) * block], attn)
        out_ref[i * block : (i + 1) * block] = attn.astype(out_ref.dtype)

    for cond, c, slot, way in sends:

        @pl.when(cond)
        def _():
            piece(c, slot, way).wait_send()


def headwise_body(
    sizes,
    lists_hbm,
    lens_hbm,
    tokens_ref,
    w_ref,
    out_ref,
    x,
    w,
    kbuf,
    vbuf,
    across,
    queries,
    results,
    got,
    weight_buf,
    total_buf,
    x_sem,
    w_sem,
    small_sem,
    send_sem,
    cross_sem,
    recv_sem,
    *small,
):
    views, halves = sizes
    view, half = lax.axis_index("view"), lax.axis_index("half")
    block, per = kbuf.shape[1:]
    local = queries.shape[1]
    inner = halves * per
    head_size = inner // HEADS
    shared = HEADS // halves
    lists, lens = small[:4], small[4:]
    slots = lists[0].shape[1]
    bufs = (kbuf, vbuf)

    loads = [
        pltpu.make_async_copy(
            tokens_ref.at[pl.ds(b * block, block)], x.at[pl.ds(b * block, block)], x_sem.at[b]
        )
        for b in range(local)
    ]
    w_loads = [
        pltpu.make_async_copy(w_ref.at[:, pl.ds(group * inner, inner)], w.at[n], w_sem.at[n])
        for n, group in enumerate((1, 2, 0))
    ]
    own_lists = [
        pltpu.make_async_copy(lists_hbm, lists[0], small_sem.at[0]),
        pltpu.make_async_copy(lens_hbm, lens[0], small_sem.at[1]),
    ]
    for load in (*loads, *w_loads, *own_lists):
        load.start()

    left = view < views // 2
    end_view = jnp.where(left, 0, views - 1)
    inner_view = jnp.where(left, 1, views - 2)
    cross_view = views - 1 - inner_view
    far_view = views - 1 - end_view
    at_end = view == end_view
    mate_view = jnp.where(at_end, inner_view, end_view)
    other = halves - 1 - half
    mate = {"view": mate_view}
    beside = {"half": other}
    diagonal = {"view": mate_view, "half": other}
    cross = {"view": cross_view}

    barrier = pltpu.get_barrier_semaphore()
    for device in (mate, diagonal):
        pl.semaphore_signal(barrier, inc=1, device_id=device, device_id_type=MESH)

    @pl.when(jnp.logical_not(at_end))
    def _():
        for device in (beside, cross):
            pl.semaphore_signal(barrier, inc=1, device_id=device, device_id_type=MESH)

    def remote(src, dst, n, kind, device):
        return pltpu.make_async_remote_copy(
            src_ref=src,
            dst_ref=dst,
            send_sem=send_sem.at[n],
            recv_sem=recv_sem.at[kind],
            device_id=device,
            device_id_type=MESH,
        )

    origins = (
        (inner_view, other),
        (end_view, half),
        (end_view, other),
        (cross_view, half),
        (cross_view, other),
        (far_view, half),
        (far_view, other),
    )
    kinds = len(origins)
    q_kind, r_kind, l_kind = 2 * kinds, 2 * kinds + 2, 2 * kinds + 4

    def span(c, of_view, of_half):
        return bufs[c].at[pl.ds((of_view * halves + of_half) * local, local)]

    def onward(c, n):
        rows = span(c, view, half) if n < 0 else span(c, *origins[n])
        return pltpu.make_async_remote_copy(
            src_ref=rows,
            dst_ref=rows,
            send_sem=cross_sem.at[c, n + 1],
            recv_sem=recv_sem.at[c * kinds + n + 4],
            device_id=cross,
            device_id_type=MESH,
        )

    def arrived(c, n):
        rows = span(c, *origins[n])
        remote(rows, rows, 0, c * kinds + n, cross).wait_recv()

    def to_row(c):
        if c < 2:
            return remote(span(c, view, half), span(c, view, half), c, c * kinds + 1, mate)
        return remote(queries.at[0], queries.at[2], c, q_kind + 1, mate)

    def to_other(c, device, origin):
        if c < 2:
            return remote(across.at[c], span(c, view, half), 3 + c, c * kinds + origin, device)
        place = 1 if origin == 0 else 3
        return remote(across.at[c], queries.at[place], 3 + c, q_kind + place - 1, device)

    def list_copies(to, n, device):
        return [
            remote(src, dst, n + j, l_kind + 2 * (to - 1) + j, device)
            for j, (src, dst) in enumerate(((lists_hbm, lists[to]), (lens_hbm, lens[to])))
        ]

    def place(c):
        w_loads[c].wait()
        for b in range(local):
            if c == 0:
                loads[b].wait()
            y = jnp.dot(
                x[b * block : (b + 1) * block], w[c], preferred_element_type=jnp.float32
            ).astype(jnp.bfloat16)
            own = jnp.where(half == 0, y[:, :per], y[:, per:])
            across[c, b] = jnp.where(half == 0, y[:, per:], y[:, :per])
            if c < 2:
                bufs[c][(view * halves + half) * local + b] = own
            else:
                queries[0, b] = own

    for c in range(3):
        place(c)
        if c == 0:
            pl.semaphore_wait(barrier, jnp.where(at_end, 2, 4))

        @pl.when(at_end)
        def _():
            to_row(c).start()
            to_other(c, diagonal, 2).start()

        @pl.when(jnp.logical_not(at_end))
        def _():
            if c < 2:
                onward(c, -1).start()
            to_other(c, beside, 0).start()

    def assemble(own, rest):
        for b in range(local):
            rows = pl.ds(b * block, block)
            out_ref[rows, :per] = jnp.where(half == 0, own[b], rest[b])
            out_ref[rows, per:] = jnp.where(half == 0, rest[b], own[b])

    head_of = lax.broadcasted_iota(jnp.int32, (block, per), 1) // head_size
    heads = [head_of == h for h in range(shared)]

    def weigh(g, i):
        q = queries[g, i]
        stacked = jnp.concatenate([jnp.where(m, q, jnp.zeros_like(q)) for m in heads], axis=0)
        keys = jnp.concatenate([kbuf[lists[g][i, s]] for s in range(slots)], axis=0)
        scores = lax.dot_general(
            stacked, keys, (((1,), (1,)), ((), ())), preferred_element_type=jnp.float32
        ) * head_size ** (-0.5)
        live = lax.broadcasted_iota(jnp.int32, scores.shape, 1) // block < lens[g][i]
        top = jnp.max(jnp.where(live, scores, NEG), axis=1, keepdims=True)
        weights = jnp.where(live, jnp.exp(scores - top), 0.0)
        total_buf[g * local + i] = jnp.sum(weights, axis=1, keepdims=True)
        weight_buf[g * local + i] = weights.astype(jnp.bfloat16)

    def finish(g, i):
        values = jnp.concatenate([vbuf[lists[g][i, s]] for s in range(slots)], axis=0)
        summed = jnp.dot(weight_buf[g * local + i], values, preferred_element_type=jnp.float32)
        scaled = summed / total_buf[g * local + i]
        attn = scaled[:block]
        for h in range(1, shared):
            attn = jnp.where(heads[h], scaled[h * block : (h + 1) * block], attn)
        results[g, i] = attn.astype(jnp.bfloat16)

    back = {
        1: remote(results.at[1], got.at[1], 6, r_kind + 1, beside),
        2: remote(results.at[2], got.at[0], 7, r_kind, mate),
        3: remote(results.at[3], got.at[1], 8, r_kind + 1, diagonal),
    }

    for load in own_lists:
        load.wait()

    @pl.when(jnp.logical_not(at_end))
    def _():
        for send in list_copies(1, 9, beside):
            send.start()
        for c in range(2):
            for n in range(3):
                arrived(c, n)
                onward(c, n).start()
        for n in range(3):
            remote(across.at[2], queries.at[n + 1], 0, q_kind + n, mate).wait_recv()
        for to in (1, 2, 3):
            for send in list_copies(to, 9, mate):
                send.wait_recv()
        for n in range(3, kinds):
            arrived(0, n)
        for g in (3, 2, 1, 0):
            for i in range(local):
                weigh(g, i)
        for n in range(3, kinds):
            arrived(1, n)
        for g in (3, 2, 1, 0):
            for i in range(local):
                finish(g, i)
            if g:
                back[g].start()
        back[1].wait_recv()
        assemble(results.at[0], got.at[1])
        for c in range(2):
            for n in range(-1, 3):
                onward(c, n).wait_send()
        for c in range(3):
            to_other(c, beside, 0).wait_send()
        for g in (1, 2, 3):
            back[g].wait_send()
        for send in list_copies(1, 9, beside):
            send.wait_send()

    @pl.when(at_end)
    def _():
        routes = (list_copies(2, 9, mate), list_copies(3, 11, diagonal))
        for route in routes:
            for send in route:
                send.start()
        back[2].wait_recv()
        back[3].wait_recv()
        assemble(got.at[0], got.at[1])
        for c in range(3):
            to_row(c).wait_send()
            to_other(c, diagonal, 2).wait_send()
        for route in routes:
            for send in route:
                send.wait_send()


def headwise(sizes, block, tokens, w_qkv, lists, lens, inner):
    views, halves = sizes
    rows, width = tokens.shape
    local, slots = lists.shape
    count, per = views * halves * local, inner // halves
    stacked = HEADS // halves * block
    anywhere = pl.BlockSpec(memory_space=pl.ANY)
    return pl.pallas_call(
        functools.partial(headwise_body, sizes),
        out_shape=pltpu.VMEM((rows, inner), jnp.bfloat16),
        in_specs=[anywhere] * 4,
        out_specs=pl.BlockSpec(memory_space=pltpu.VMEM),
        scratch_shapes=[
            pltpu.VMEM((rows, width), jnp.bfloat16),
            pltpu.VMEM((3, width, inner), jnp.bfloat16),
            pltpu.VMEM((count, block, per), jnp.bfloat16),
            pltpu.VMEM((count, block, per), jnp.bfloat16),
            pltpu.VMEM((3, local, block, per), jnp.bfloat16),
            pltpu.VMEM((4, local, block, per), jnp.bfloat16),
            pltpu.VMEM((4, local, block, per), jnp.bfloat16),
            pltpu.VMEM((2, local, block, per), jnp.bfloat16),
            pltpu.VMEM((4 * local, stacked, slots * block), jnp.bfloat16),
            pltpu.VMEM((4 * local, stacked, 1), jnp.float32),
            pltpu.SemaphoreType.DMA((local,)),
            pltpu.SemaphoreType.DMA((3,)),
            pltpu.SemaphoreType.DMA((2,)),
            pltpu.SemaphoreType.DMA((13,)),
            pltpu.SemaphoreType.DMA((2, 4)),
            pltpu.SemaphoreType.DMA((25,)),
            *[pltpu.SMEM((local, slots), jnp.int32)] * 4,
            *[pltpu.SMEM((local,), jnp.int32)] * 4,
        ],
        compiler_params=pltpu.CompilerParams(
            collective_id=0, has_side_effects=True, vmem_limit_bytes=62000000
        ),
    )(lists, lens, tokens, w_qkv)


def project_out(attn, w_out):
    mixed = jnp.dot(attn, w_out, preferred_element_type=jnp.float32).astype(jnp.bfloat16)
    return mixed.reshape(1, *mixed.shape)


def per_device(sizes, tokens, w_qkv, w_out, key_lists, list_len):
    views, halves = sizes
    rows, width = tokens.shape[1:]
    inner = w_out.shape[0]
    local = key_lists.shape[1]
    slots = key_lists.shape[2]
    block = rows // local
    shards = views * halves
    if views == 4 and halves == 2:
        attn = headwise(
            sizes,
            block,
            tokens.reshape(rows, width),
            w_qkv,
            key_lists.reshape(local, slots),
            list_len.reshape(local),
            inner,
        )
        return project_out(attn, w_out)
    anywhere = pl.BlockSpec(memory_space=pl.ANY)
    attn = pl.pallas_call(
        functools.partial(body, sizes),
        out_shape=pltpu.VMEM((rows, inner), jnp.bfloat16),
        in_specs=[
            anywhere,
            anywhere,
            anywhere,
            anywhere,
        ],
        out_specs=pl.BlockSpec(memory_space=pltpu.VMEM),
        scratch_shapes=[
            pltpu.VMEM((rows, width), jnp.bfloat16),
            pltpu.VMEM((3, width, inner), jnp.bfloat16),
            pltpu.VMEM((shards * local, block, inner), jnp.bfloat16),
            pltpu.VMEM((shards * local, block, inner), jnp.bfloat16),
            pltpu.VMEM((local, HEADS * block, slots * block), jnp.bfloat16),
            pltpu.VMEM((local, HEADS * block, 1), jnp.float32),
            pltpu.SemaphoreType.DMA((4,)),
            pltpu.SemaphoreType.DMA((4, 2, shards * local)),
            pltpu.SemaphoreType.DMA((2, shards * local)),
            pltpu.SMEM((local, slots), jnp.int32),
            pltpu.SMEM((local,), jnp.int32),
            pltpu.SemaphoreType.DMA((2,)),
            pltpu.SemaphoreType.DMA((local,)),
        ],
        compiler_params=pltpu.CompilerParams(collective_id=0, has_side_effects=True, vmem_limit_bytes=62000000),
    )(
        key_lists.reshape(local, slots),
        list_len.reshape(local),
        tokens.reshape(rows, width),
        w_qkv,
    )
    return project_out(attn, w_out)


def solution(mesh):
    sizes = (mesh.shape["view"], mesh.shape["half"])
    placed = (
        P(("scene", "view"), "half", None),
        P(),
        P(),
        P(("scene", "view"), "half", None),
        P(("scene", "view"), "half"),
    )
    return jax.shard_map(
        functools.partial(per_device, sizes),
        mesh=mesh,
        in_specs=placed,
        out_specs=P(("scene", "view"), "half", None),
        check_vma=False,
    )
```

```python
import functools

import jax
import jax.numpy as jnp
from jax import lax
from jax.experimental import pallas as pl
from jax.experimental.pallas import tpu as pltpu
from jax.sharding import PartitionSpec as P

HEADS = 4
NEG = -1e30
STEPS = 4
MESH = pl.DeviceIdType.MESH


def body(
    sizes,
    lists_hbm,
    lens_hbm,
    tokens_ref,
    w_ref,
    out_ref,
    x,
    w,
    kbuf,
    vbuf,
    weight_buf,
    total_buf,
    load_sem,
    send_sem,
    recv_sem,
    lists_ref,
    lens_ref,
    small_sem,
    xsem,
):
    views, halves = sizes
    view, half = lax.axis_index("view"), lax.axis_index("half")
    count, block, inner = kbuf.shape
    local = count // (views * halves)
    rows = local * block
    head_size = inner // HEADS
    slots = lists_ref.shape[1]
    small = [pltpu.make_async_copy(lists_hbm, lists_ref, small_sem.at[0]), pltpu.make_async_copy(lens_hbm, lens_ref, small_sem.at[1])]
    bufs = (kbuf, vbuf)

    loads = []
    for n, group in enumerate((1, 2, 0)):
        cols = pl.ds(group * inner, inner)
        loads.append(
            pltpu.make_async_copy(w_ref.at[:, cols], w.at[group], load_sem.at[n])
        )
    xl = [pltpu.make_async_copy(tokens_ref.at[pl.ds(b * block, block)], x.at[pl.ds(b * block, block)], xsem.at[b]) for b in range(local)]
    xl[0].start()
    loads[0].start()
    for l in xl[1:]:
        l.start()
    for l in loads[1:]:
        l.start()
    for cp in small:
        cp.start()

    toward = (
        (view + 1 < views, {"view": view + 1}, views),
        (view >= 1, {"view": view - 1}, views),
        (half + 1 < halves, {"half": half + 1}, halves),
        (half >= 1, {"half": half - 1}, halves),
    )

    barrier = pltpu.get_barrier_semaphore()
    for there, device, size in toward:
        if size > 1:

            @pl.when(there)
            def _():
                pl.semaphore_signal(barrier, inc=1, device_id=device, device_id_type=MESH)

    def piece(c, slot, way):
        rows_of = bufs[c].at[slot]
        return pltpu.make_async_remote_copy(
            src_ref=rows_of,
            dst_ref=rows_of,
            send_sem=send_sem.at[way, c, slot],
            recv_sem=recv_sem.at[c, slot],
            device_id=toward[way][1],
            device_id_type=MESH,
        )

    sends = []

    def send(c, slot, way, here):
        there, _, size = toward[way]
        if size == 1:
            return
        cond = there if here is None else jnp.logical_and(here, there)
        sends.append((cond, c, slot, way))

        @pl.when(cond)
        def _():
            piece(c, slot, way).start()

    def arrive(c, slot, here):
        @pl.when(here)
        def _():
            piece(c, slot, 0).wait_recv()

    def project(group):
        return jnp.dot(x[...], w[group], preferred_element_type=jnp.float32).astype(
            jnp.bfloat16
        )

    own = view * halves + half
    for c in range(2):
        loads[c].wait()
        for b in range(local):
            if c == 0:
                xl[b].wait()
            bufs[c][own * local + b] = jnp.dot(
                x[b * block : (b + 1) * block], w[1 + c], preferred_element_type=jnp.float32
            ).astype(jnp.bfloat16)
            if c == 0 and b == 0:
                expected = sum(there.astype(jnp.int32) for there, _, size in toward if size > 1)
                pl.semaphore_wait(barrier, expected)
            for way in (2, 3, 0, 1):
                send(c, own * local + b, way, None)

    loads[2].wait()
    for cp in small:
        cp.wait()
    queries = project(0)
    head_of = lax.broadcasted_iota(jnp.int32, (block, inner), 1) // head_size
    mine = [head_of == h for h in range(HEADS)]

    balanced = halves == 2 and views > 2
    last = views - 1

    def along_view(c, dist):
        for b in range(local):
            for sign, way in ((-1, 0), (1, 1)):
                shard = view + sign * dist
                here = shard >= 0 if sign < 0 else shard < views
                slot = (shard * halves + half) * local + b
                arrive(c, slot, here)
                across = here
                if balanced and c == 1:
                    across = shard >= 1 if sign < 0 else shard < last
                for out in (2, 3):
                    send(c, slot, out, across)
                if dist + 1 < views:
                    send(c, slot, way, here)

    def relay(dist):
        for b in range(local):
            for shard, here, way in ((0, view == dist, 0), (last, view == last - dist, 1)):
                slot = (shard * halves + (halves - 1) - half) * local + b
                arrive(1, slot, here)
                if dist < last:
                    send(1, slot, way, here)

    def along_half(c):
        for far in range(1, halves):
            for dist in range(views):
                for b in range(local):
                    for sign in (-1, 1) if dist else (1,):
                        shard = view + sign * dist
                        seen = shard >= 0 if sign < 0 else shard < views
                        if balanced and c == 1:
                            seen = jnp.logical_and(shard >= 1, shard < last)
                        for side, way in ((-1, 2), (1, 3)):
                            other = half + side * far
                            here = jnp.logical_and(
                                seen, other >= 0 if side < 0 else other < halves
                            )
                            slot = (shard * halves + other) * local + b
                            arrive(c, slot, here)
                            if far + 1 < halves:
                                send(c, slot, way, here)

    for dist in range(1, views):
        along_view(0, dist)
        if balanced and dist > 1:
            relay(dist - 1)
        along_view(1, dist)
        if balanced and dist == 1:
            relay(0)

    along_half(0)
    for i in range(local):
        q = queries[i * block : (i + 1) * block]
        stacked = jnp.concatenate([jnp.where(m, q, jnp.zeros_like(q)) for m in mine], axis=0)
        keys = jnp.concatenate([kbuf[lists_ref[i, s]] for s in range(slots)], axis=0)
        scores = lax.dot_general(
            stacked, keys, (((1,), (1,)), ((), ())), preferred_element_type=jnp.float32
        ) * head_size ** (-0.5)
        live = lax.broadcasted_iota(jnp.int32, scores.shape, 1) // block < lens_ref[i]
        top = jnp.max(jnp.where(live, scores, NEG), axis=1, keepdims=True)
        weights = jnp.where(live, jnp.exp(scores - top), 0.0)
        total_buf[i] = jnp.sum(weights, axis=1, keepdims=True)
        weight_buf[i] = weights.astype(jnp.bfloat16)

    along_half(1)
    if balanced:
        relay(last)
    for i in range(local):
        values = jnp.concatenate([vbuf[lists_ref[i, s]] for s in range(slots)], axis=0)
        summed = jnp.dot(weight_buf[i], values, preferred_element_type=jnp.float32)
        scaled = summed / total_buf[i]
        attn = jnp.zeros((block, inner), jnp.float32)
        for h, m in enumerate(mine):
            attn = jnp.where(m, scaled[h * block : (h + 1) * block], attn)
        out_ref[i * block : (i + 1) * block] = attn.astype(out_ref.dtype)

    for cond, c, slot, way in sends:

        @pl.when(cond)
        def _():
            piece(c, slot, way).wait_send()


def headwise_body(
    sizes,
    lists_hbm,
    lens_hbm,
    tokens_ref,
    w_ref,
    out_ref,
    x,
    w,
    kbuf,
    vbuf,
    across,
    queries,
    results,
    got,
    weight_buf,
    total_buf,
    x_sem,
    w_sem,
    small_sem,
    send_sem,
    cross_sem,
    recv_sem,
    *small,
):
    views, halves = sizes
    steps = x_sem.shape[0]
    view, half = lax.axis_index("view"), lax.axis_index("half")
    block, per = kbuf.shape[1:]
    local = queries.shape[1]
    inner = halves * per
    head_size = inner // HEADS
    shared = HEADS // halves
    lists, lens = small[:4], small[4:]
    slots = lists[0].shape[1]
    bufs = (kbuf, vbuf)

    depth = x.shape[1] // steps
    parts = [pl.ds(n * depth, depth) for n in range(steps)]
    loads = [
        pltpu.make_async_copy(tokens_ref.at[:, part], x.at[:, part], x_sem.at[n])
        for n, part in enumerate(parts)
    ]
    columns = [pl.ds(group * inner, inner) for group in (1, 2, 0)]
    key_loads = [
        pltpu.make_async_copy(w_ref.at[part, columns[0]], w.at[0, part], w_sem.at[2 + n])
        for n, part in enumerate(parts)
    ]
    w_loads = [
        pltpu.make_async_copy(w_ref.at[:, columns[c]], w.at[c], w_sem.at[c - 1]) for c in (1, 2)
    ]
    own_lists = [
        pltpu.make_async_copy(lists_hbm, lists[0], small_sem.at[0]),
        pltpu.make_async_copy(lens_hbm, lens[0], small_sem.at[1]),
    ]
    for pair in zip(loads, key_loads):
        for load in pair:
            load.start()
    for load in (*w_loads, *own_lists):
        load.start()

    left = view < views // 2
    end_view = jnp.where(left, 0, views - 1)
    inner_view = jnp.where(left, 1, views - 2)
    cross_view = views - 1 - inner_view
    far_view = views - 1 - end_view
    at_end = view == end_view
    mate_view = jnp.where(at_end, inner_view, end_view)
    other = halves - 1 - half
    mate = {"view": mate_view}
    beside = {"half": other}
    diagonal = {"view": mate_view, "half": other}
    cross = {"view": cross_view}

    barrier = pltpu.get_barrier_semaphore()
    for device in (mate, diagonal):
        pl.semaphore_signal(barrier, inc=1, device_id=device, device_id_type=MESH)

    @pl.when(jnp.logical_not(at_end))
    def _():
        for device in (beside, cross):
            pl.semaphore_signal(barrier, inc=1, device_id=device, device_id_type=MESH)

    def remote(src, dst, n, kind, device):
        return pltpu.make_async_remote_copy(
            src_ref=src,
            dst_ref=dst,
            send_sem=send_sem.at[n],
            recv_sem=recv_sem.at[kind],
            device_id=device,
            device_id_type=MESH,
        )

    origins = (
        (inner_view, other),
        (end_view, half),
        (end_view, other),
        (cross_view, half),
        (cross_view, other),
        (far_view, half),
        (far_view, other),
    )
    kinds = len(origins)
    q_kind, r_kind, l_kind = 2 * kinds, 2 * kinds + 2, 2 * kinds + 4

    def span(c, of_view, of_half):
        return bufs[c].at[pl.ds((of_view * halves + of_half) * local, local)]

    def onward(c, n):
        rows = span(c, view, half) if n < 0 else span(c, *origins[n])
        return pltpu.make_async_remote_copy(
            src_ref=rows,
            dst_ref=rows,
            send_sem=cross_sem.at[c, n + 1],
            recv_sem=recv_sem.at[c * kinds + n + 4],
            device_id=cross,
            device_id_type=MESH,
        )

    def arrived(c, n):
        rows = span(c, *origins[n])
        remote(rows, rows, 0, c * kinds + n, cross).wait_recv()

    def to_row(c):
        if c < 2:
            return remote(span(c, view, half), span(c, view, half), c, c * kinds + 1, mate)
        return remote(queries.at[0], queries.at[2], c, q_kind + 1, mate)

    def to_other(c, device, origin):
        if c < 2:
            return remote(across.at[c], span(c, view, half), 3 + c, c * kinds + origin, device)
        place = 1 if origin == 0 else 3
        return remote(across.at[c], queries.at[place], 3 + c, q_kind + place - 1, device)

    def list_copies(to, n, device):
        return [
            remote(src, dst, n + j, l_kind + 2 * (to - 1) + j, device)
            for j, (src, dst) in enumerate(((lists_hbm, lists[to]), (lens_hbm, lens[to])))
        ]

    def place(c):
        if c == 0:
            y = jnp.zeros((local * block, inner), jnp.float32)
            for n, part in enumerate(parts):
                loads[n].wait()
                key_loads[n].wait()
                y += jnp.dot(x[:, part], w[c, part], preferred_element_type=jnp.float32)
        else:
            w_loads[c - 1].wait()
            y = jnp.dot(x[...], w[c], preferred_element_type=jnp.float32)
        y = y.astype(jnp.bfloat16)
        for b in range(local):
            rows = y[b * block : (b + 1) * block]
            own = jnp.where(half == 0, rows[:, :per], rows[:, per:])
            across[c, b] = jnp.where(half == 0, rows[:, per:], rows[:, :per])
            if c < 2:
                bufs[c][(view * halves + half) * local + b] = own
            else:
                queries[0, b] = own

    for c in range(3):
        place(c)
        if c == 0:
            pl.semaphore_wait(barrier, jnp.where(at_end, 2, 4))

        @pl.when(at_end)
        def _():
            to_row(c).start()
            to_other(c, diagonal, 2).start()

        @pl.when(jnp.logical_not(at_end))
        def _():
            if c < 1:
                onward(c, -1).start()
            to_other(c, beside, 0).start()
            if c == 1:
                onward(c, -1).start()

    def assemble(own, rest):
        for b in range(local):
            rows = pl.ds(b * block, block)
            out_ref[rows, :per] = jnp.where(half == 0, own[b], rest[b])
            out_ref[rows, per:] = jnp.where(half == 0, rest[b], own[b])

    head_of = lax.broadcasted_iota(jnp.int32, (block, per), 1) // head_size
    heads = [head_of == h for h in range(shared)]

    def weigh(g, i):
        q = queries[g, i]
        stacked = jnp.concatenate([jnp.where(m, q, jnp.zeros_like(q)) for m in heads], axis=0)
        keys = jnp.concatenate([kbuf[lists[g][i, s]] for s in range(slots)], axis=0)
        scores = lax.dot_general(
            stacked, keys, (((1,), (1,)), ((), ())), preferred_element_type=jnp.float32
        ) * head_size ** (-0.5)
        live = lax.broadcasted_iota(jnp.int32, scores.shape, 1) // block < lens[g][i]
        top = jnp.max(jnp.where(live, scores, NEG), axis=1, keepdims=True)
        weights = jnp.where(live, jnp.exp(scores - top), 0.0)
        total_buf[g * local + i] = jnp.sum(weights, axis=1, keepdims=True)
        weight_buf[g * local + i] = weights.astype(jnp.bfloat16)

    def finish(g, i):
        values = jnp.concatenate([vbuf[lists[g][i, s]] for s in range(slots)], axis=0)
        summed = jnp.dot(weight_buf[g * local + i], values, preferred_element_type=jnp.float32)
        scaled = summed / total_buf[g * local + i]
        attn = scaled[:block]
        for h in range(1, shared):
            attn = jnp.where(heads[h], scaled[h * block : (h + 1) * block], attn)
        results[g, i] = attn.astype(jnp.bfloat16)

    back = {
        1: remote(results.at[1], got.at[1], 6, r_kind + 1, beside),
        2: remote(results.at[2], got.at[0], 7, r_kind, mate),
        3: remote(results.at[3], got.at[1], 8, r_kind + 1, diagonal),
    }

    for load in own_lists:
        load.wait()

    @pl.when(jnp.logical_not(at_end))
    def _():
        for send in list_copies(1, 9, beside):
            send.start()
        for c, n in ((0, 0), (0, 1), (0, 2), (1, 0), (1, 1), (1, 2)):
            arrived(c, n)
            onward(c, n).start()
        for n in range(3):
            remote(across.at[2], queries.at[n + 1], 0, q_kind + n, mate).wait_recv()
        for to in (1, 2, 3):
            for send in list_copies(to, 9, mate):
                send.wait_recv()
        for n in range(3, kinds):
            arrived(0, n)
        for g in (3, 2, 1, 0):
            for i in range(local):
                weigh(g, i)
        for n in range(3, kinds):
            arrived(1, n)
        for first, order in ((0, (2, 3)), (1, (3, 2))):

            @pl.when(half == first)
            def _():
                for g in order:
                    for i in range(local):
                        finish(g, i)
                    back[g].start()

        for g in (1, 0):
            for i in range(local):
                finish(g, i)
            if g:
                back[g].start()
        back[1].wait_recv()
        assemble(results.at[0], got.at[1])
        for c in range(2):
            for n in range(-1, 3):
                onward(c, n).wait_send()
        for c in range(3):
            to_other(c, beside, 0).wait_send()
        for g in (1, 2, 3):
            back[g].wait_send()
        for send in list_copies(1, 9, beside):
            send.wait_send()

    @pl.when(at_end)
    def _():
        routes = (list_copies(2, 9, mate), list_copies(3, 11, diagonal))
        for route in routes:
            for send in route:
                send.start()
        back[2].wait_recv()
        back[3].wait_recv()
        assemble(got.at[0], got.at[1])
        for c in range(3):
            to_row(c).wait_send()
            to_other(c, diagonal, 2).wait_send()
        for route in routes:
            for send in route:
                send.wait_send()


def headwise(sizes, block, tokens, w_qkv, lists, lens, inner):
    views, halves = sizes
    rows, width = tokens.shape
    local, slots = lists.shape
    count, per = views * halves * local, inner // halves
    stacked = HEADS // halves * block
    anywhere = pl.BlockSpec(memory_space=pl.ANY)
    return pl.pallas_call(
        functools.partial(headwise_body, sizes),
        out_shape=pltpu.VMEM((rows, inner), jnp.bfloat16),
        in_specs=[anywhere] * 4,
        out_specs=pl.BlockSpec(memory_space=pltpu.VMEM),
        scratch_shapes=[
            pltpu.VMEM((rows, width), jnp.bfloat16),
            pltpu.VMEM((3, width, inner), jnp.bfloat16),
            pltpu.VMEM((count, block, per), jnp.bfloat16),
            pltpu.VMEM((count, block, per), jnp.bfloat16),
            pltpu.VMEM((3, local, block, per), jnp.bfloat16),
            pltpu.VMEM((4, local, block, per), jnp.bfloat16),
            pltpu.VMEM((4, local, block, per), jnp.bfloat16),
            pltpu.VMEM((2, local, block, per), jnp.bfloat16),
            pltpu.VMEM((4 * local, stacked, slots * block), jnp.bfloat16),
            pltpu.VMEM((4 * local, stacked, 1), jnp.float32),
            pltpu.SemaphoreType.DMA((STEPS,)),
            pltpu.SemaphoreType.DMA((2 + STEPS,)),
            pltpu.SemaphoreType.DMA((2,)),
            pltpu.SemaphoreType.DMA((13,)),
            pltpu.SemaphoreType.DMA((2, 4)),
            pltpu.SemaphoreType.DMA((25,)),
            *[pltpu.SMEM((local, slots), jnp.int32)] * 4,
            *[pltpu.SMEM((local,), jnp.int32)] * 4,
        ],
        compiler_params=pltpu.CompilerParams(
            collective_id=0, has_side_effects=True, vmem_limit_bytes=62000000
        ),
    )(lists, lens, tokens, w_qkv)


def mix_body(attn_ref, w_ref, out_ref, buf, sem):
    width = out_ref.shape[1]
    step = width // 4
    copies = []
    for n in range(4):
        cols = pl.ds(n * step, step)
        buf[n] = jnp.dot(
            attn_ref[...], w_ref[:, cols], preferred_element_type=jnp.float32
        ).astype(jnp.bfloat16)
        copies.append(pltpu.make_async_copy(buf.at[n], out_ref.at[:, cols], sem.at[n]))
        copies[-1].start()
    for copy in copies:
        copy.wait()


def project_out(attn, w_out):
    rows, width = attn.shape[0], w_out.shape[1]
    mixed = pl.pallas_call(
        mix_body,
        out_shape=jax.ShapeDtypeStruct((rows, width), jnp.bfloat16),
        in_specs=[pl.BlockSpec(memory_space=pltpu.VMEM), pl.BlockSpec(memory_space=pltpu.VMEM)],
        out_specs=pl.BlockSpec(memory_space=pl.ANY),
        scratch_shapes=[pltpu.VMEM((4, rows, width // 4), jnp.bfloat16), pltpu.SemaphoreType.DMA((4,))],
        compiler_params=pltpu.CompilerParams(vmem_limit_bytes=16000000),
    )(attn, w_out)
    return mixed.reshape(1, rows, width)


def per_device(sizes, tokens, w_qkv, w_out, key_lists, list_len):
    views, halves = sizes
    rows, width = tokens.shape[1:]
    inner = w_out.shape[0]
    local = key_lists.shape[1]
    slots = key_lists.shape[2]
    block = rows // local
    shards = views * halves
    if views == 4 and halves == 2:
        attn = headwise(
            sizes,
            block,
            tokens.reshape(rows, width),
            w_qkv,
            key_lists.reshape(local, slots),
            list_len.reshape(local),
            inner,
        )
        return project_out(attn, w_out)
    anywhere = pl.BlockSpec(memory_space=pl.ANY)
    attn = pl.pallas_call(
        functools.partial(body, sizes),
        out_shape=pltpu.VMEM((rows, inner), jnp.bfloat16),
        in_specs=[
            anywhere,
            anywhere,
            anywhere,
            anywhere,
        ],
        out_specs=pl.BlockSpec(memory_space=pltpu.VMEM),
        scratch_shapes=[
            pltpu.VMEM((rows, width), jnp.bfloat16),
            pltpu.VMEM((3, width, inner), jnp.bfloat16),
            pltpu.VMEM((shards * local, block, inner), jnp.bfloat16),
            pltpu.VMEM((shards * local, block, inner), jnp.bfloat16),
            pltpu.VMEM((local, HEADS * block, slots * block), jnp.bfloat16),
            pltpu.VMEM((local, HEADS * block, 1), jnp.float32),
            pltpu.SemaphoreType.DMA((4,)),
            pltpu.SemaphoreType.DMA((4, 2, shards * local)),
            pltpu.SemaphoreType.DMA((2, shards * local)),
            pltpu.SMEM((local, slots), jnp.int32),
            pltpu.SMEM((local,), jnp.int32),
            pltpu.SemaphoreType.DMA((2,)),
            pltpu.SemaphoreType.DMA((local,)),
        ],
        compiler_params=pltpu.CompilerParams(collective_id=0, has_side_effects=True, vmem_limit_bytes=62000000),
    )(
        key_lists.reshape(local, slots),
        list_len.reshape(local),
        tokens.reshape(rows, width),
        w_qkv,
    )
    return project_out(attn, w_out)


def solution(mesh):
    sizes = (mesh.shape["view"], mesh.shape["half"])
    placed = (
        P(("scene", "view"), "half", None),
        P(),
        P(),
        P(("scene", "view"), "half", None),
        P(("scene", "view"), "half"),
    )
    return jax.shard_map(
        functools.partial(per_device, sizes),
        mesh=mesh,
        in_specs=placed,
        out_specs=P(("scene", "view"), "half", None),
        check_vma=False,
    )
```

```python
import functools

import jax
import jax.numpy as jnp
from jax import lax
from jax.experimental import pallas as pl
from jax.experimental.pallas import tpu as pltpu
from jax.sharding import PartitionSpec as P

HEADS = 4
NEG = -1e30
STEPS = 4
MESH = pl.DeviceIdType.MESH


def body(
    sizes,
    lists_hbm,
    lens_hbm,
    tokens_ref,
    w_ref,
    out_ref,
    x,
    w,
    kbuf,
    vbuf,
    weight_buf,
    total_buf,
    load_sem,
    send_sem,
    recv_sem,
    lists_ref,
    lens_ref,
    small_sem,
    xsem,
):
    views, halves = sizes
    view, half = lax.axis_index("view"), lax.axis_index("half")
    count, block, inner = kbuf.shape
    local = count // (views * halves)
    rows = local * block
    head_size = inner // HEADS
    slots = lists_ref.shape[1]
    small = [pltpu.make_async_copy(lists_hbm, lists_ref, small_sem.at[0]), pltpu.make_async_copy(lens_hbm, lens_ref, small_sem.at[1])]
    bufs = (kbuf, vbuf)

    loads = []
    for n, group in enumerate((1, 2, 0)):
        cols = pl.ds(group * inner, inner)
        loads.append(
            pltpu.make_async_copy(w_ref.at[:, cols], w.at[group], load_sem.at[n])
        )
    xl = [pltpu.make_async_copy(tokens_ref.at[pl.ds(b * block, block)], x.at[pl.ds(b * block, block)], xsem.at[b]) for b in range(local)]
    xl[0].start()
    loads[0].start()
    for l in xl[1:]:
        l.start()
    for l in loads[1:]:
        l.start()
    for cp in small:
        cp.start()

    toward = (
        (view + 1 < views, {"view": view + 1}, views),
        (view >= 1, {"view": view - 1}, views),
        (half + 1 < halves, {"half": half + 1}, halves),
        (half >= 1, {"half": half - 1}, halves),
    )

    barrier = pltpu.get_barrier_semaphore()
    for there, device, size in toward:
        if size > 1:

            @pl.when(there)
            def _():
                pl.semaphore_signal(barrier, inc=1, device_id=device, device_id_type=MESH)

    def piece(c, slot, way):
        rows_of = bufs[c].at[slot]
        return pltpu.make_async_remote_copy(
            src_ref=rows_of,
            dst_ref=rows_of,
            send_sem=send_sem.at[way, c, slot],
            recv_sem=recv_sem.at[c, slot],
            device_id=toward[way][1],
            device_id_type=MESH,
        )

    sends = []

    def send(c, slot, way, here):
        there, _, size = toward[way]
        if size == 1:
            return
        cond = there if here is None else jnp.logical_and(here, there)
        sends.append((cond, c, slot, way))

        @pl.when(cond)
        def _():
            piece(c, slot, way).start()

    def arrive(c, slot, here):
        @pl.when(here)
        def _():
            piece(c, slot, 0).wait_recv()

    def project(group):
        return jnp.dot(x[...], w[group], preferred_element_type=jnp.float32).astype(
            jnp.bfloat16
        )

    own = view * halves + half
    for c in range(2):
        loads[c].wait()
        for b in range(local):
            if c == 0:
                xl[b].wait()
            bufs[c][own * local + b] = jnp.dot(
                x[b * block : (b + 1) * block], w[1 + c], preferred_element_type=jnp.float32
            ).astype(jnp.bfloat16)
            if c == 0 and b == 0:
                expected = sum(there.astype(jnp.int32) for there, _, size in toward if size > 1)
                pl.semaphore_wait(barrier, expected)
            for way in (2, 3, 0, 1):
                send(c, own * local + b, way, None)

    loads[2].wait()
    for cp in small:
        cp.wait()
    queries = project(0)
    head_of = lax.broadcasted_iota(jnp.int32, (block, inner), 1) // head_size
    mine = [head_of == h for h in range(HEADS)]

    balanced = halves == 2 and views > 2
    last = views - 1

    def along_view(c, dist):
        for b in range(local):
            for sign, way in ((-1, 0), (1, 1)):
                shard = view + sign * dist
                here = shard >= 0 if sign < 0 else shard < views
                slot = (shard * halves + half) * local + b
                arrive(c, slot, here)
                across = here
                if balanced and c == 1:
                    across = shard >= 1 if sign < 0 else shard < last
                for out in (2, 3):
                    send(c, slot, out, across)
                if dist + 1 < views:
                    send(c, slot, way, here)

    def relay(dist):
        for b in range(local):
            for shard, here, way in ((0, view == dist, 0), (last, view == last - dist, 1)):
                slot = (shard * halves + (halves - 1) - half) * local + b
                arrive(1, slot, here)
                if dist < last:
                    send(1, slot, way, here)

    def along_half(c):
        for far in range(1, halves):
            for dist in range(views):
                for b in range(local):
                    for sign in (-1, 1) if dist else (1,):
                        shard = view + sign * dist
                        seen = shard >= 0 if sign < 0 else shard < views
                        if balanced and c == 1:
                            seen = jnp.logical_and(shard >= 1, shard < last)
                        for side, way in ((-1, 2), (1, 3)):
                            other = half + side * far
                            here = jnp.logical_and(
                                seen, other >= 0 if side < 0 else other < halves
                            )
                            slot = (shard * halves + other) * local + b
                            arrive(c, slot, here)
                            if far + 1 < halves:
                                send(c, slot, way, here)

    for dist in range(1, views):
        along_view(0, dist)
        if balanced and dist > 1:
            relay(dist - 1)
        along_view(1, dist)
        if balanced and dist == 1:
            relay(0)

    along_half(0)
    for i in range(local):
        q = queries[i * block : (i + 1) * block]
        stacked = jnp.concatenate([jnp.where(m, q, jnp.zeros_like(q)) for m in mine], axis=0)
        keys = jnp.concatenate([kbuf[lists_ref[i, s]] for s in range(slots)], axis=0)
        scores = lax.dot_general(
            stacked, keys, (((1,), (1,)), ((), ())), preferred_element_type=jnp.float32
        ) * head_size ** (-0.5)
        live = lax.broadcasted_iota(jnp.int32, scores.shape, 1) // block < lens_ref[i]
        top = jnp.max(jnp.where(live, scores, NEG), axis=1, keepdims=True)
        weights = jnp.where(live, jnp.exp(scores - top), 0.0)
        total_buf[i] = jnp.sum(weights, axis=1, keepdims=True)
        weight_buf[i] = weights.astype(jnp.bfloat16)

    along_half(1)
    if balanced:
        relay(last)
    for i in range(local):
        values = jnp.concatenate([vbuf[lists_ref[i, s]] for s in range(slots)], axis=0)
        summed = jnp.dot(weight_buf[i], values, preferred_element_type=jnp.float32)
        scaled = summed / total_buf[i]
        attn = jnp.zeros((block, inner), jnp.float32)
        for h, m in enumerate(mine):
            attn = jnp.where(m, scaled[h * block : (h + 1) * block], attn)
        out_ref[i * block : (i + 1) * block] = attn.astype(out_ref.dtype)

    for cond, c, slot, way in sends:

        @pl.when(cond)
        def _():
            piece(c, slot, way).wait_send()


def headwise_body(
    sizes,
    lists_hbm,
    lens_hbm,
    tokens_ref,
    w_ref,
    out_ref,
    x,
    w,
    kbuf,
    vbuf,
    across,
    queries,
    results,
    got,
    weight_buf,
    total_buf,
    x_sem,
    w_sem,
    small_sem,
    send_sem,
    cross_sem,
    recv_sem,
    *small,
):
    views, halves = sizes
    steps = x_sem.shape[0]
    view, half = lax.axis_index("view"), lax.axis_index("half")
    block, per = kbuf.shape[1:]
    local = queries.shape[1]
    inner = halves * per
    head_size = inner // HEADS
    shared = HEADS // halves
    lists, lens = small[:4], small[4:]
    slots = lists[0].shape[1]
    bufs = (kbuf, vbuf)

    depth = x.shape[1] // steps
    parts = [pl.ds(n * depth, depth) for n in range(steps)]
    loads = [
        pltpu.make_async_copy(tokens_ref.at[:, part], x.at[:, part], x_sem.at[n])
        for n, part in enumerate(parts)
    ]
    columns = [pl.ds(group * inner, inner) for group in (1, 2, 0)]
    key_loads = [
        pltpu.make_async_copy(w_ref.at[part, columns[0]], w.at[0, part], w_sem.at[2 + n])
        for n, part in enumerate(parts)
    ]
    w_loads = [
        pltpu.make_async_copy(w_ref.at[:, columns[c]], w.at[c], w_sem.at[c - 1]) for c in (1, 2)
    ]
    own_lists = [
        pltpu.make_async_copy(lists_hbm, lists[0], small_sem.at[0]),
        pltpu.make_async_copy(lens_hbm, lens[0], small_sem.at[1]),
    ]
    for pair in zip(loads, key_loads):
        for load in pair:
            load.start()
    for load in (*w_loads, *own_lists):
        load.start()

    left = view < views // 2
    end_view = jnp.where(left, 0, views - 1)
    inner_view = jnp.where(left, 1, views - 2)
    cross_view = views - 1 - inner_view
    far_view = views - 1 - end_view
    at_end = view == end_view
    mate_view = jnp.where(at_end, inner_view, end_view)
    other = halves - 1 - half
    mate = {"view": mate_view}
    beside = {"half": other}
    diagonal = {"view": mate_view, "half": other}
    cross = {"view": cross_view}

    barrier = pltpu.get_barrier_semaphore()
    for device in (mate, diagonal):
        pl.semaphore_signal(barrier, inc=1, device_id=device, device_id_type=MESH)

    @pl.when(jnp.logical_not(at_end))
    def _():
        for device in (beside, cross):
            pl.semaphore_signal(barrier, inc=1, device_id=device, device_id_type=MESH)

    def remote(src, dst, n, kind, device):
        return pltpu.make_async_remote_copy(
            src_ref=src,
            dst_ref=dst,
            send_sem=send_sem.at[n],
            recv_sem=recv_sem.at[kind],
            device_id=device,
            device_id_type=MESH,
        )

    origins = (
        (inner_view, other),
        (end_view, half),
        (end_view, other),
        (cross_view, half),
        (cross_view, other),
        (far_view, half),
        (far_view, other),
    )
    kinds = len(origins)
    q_kind, r_kind, l_kind = 2 * kinds, 2 * kinds + 2, 2 * kinds + 4

    def span(c, of_view, of_half):
        return bufs[c].at[pl.ds((of_view * halves + of_half) * local, local)]

    def onward(c, n):
        rows = span(c, view, half) if n < 0 else span(c, *origins[n])
        return pltpu.make_async_remote_copy(
            src_ref=rows,
            dst_ref=rows,
            send_sem=cross_sem.at[c, n + 1],
            recv_sem=recv_sem.at[c * kinds + n + 4],
            device_id=cross,
            device_id_type=MESH,
        )

    def arrived(c, n):
        rows = span(c, *origins[n])
        remote(rows, rows, 0, c * kinds + n, cross).wait_recv()

    def to_row(c):
        if c < 2:
            return remote(span(c, view, half), span(c, view, half), c, c * kinds + 1, mate)
        return remote(queries.at[0], queries.at[2], c, q_kind + 1, mate)

    def to_other(c, device, origin):
        if c < 2:
            return remote(across.at[c], span(c, view, half), 3 + c, c * kinds + origin, device)
        place = 1 if origin == 0 else 3
        return remote(across.at[c], queries.at[place], 3 + c, q_kind + place - 1, device)

    def list_copies(to, n, device):
        return [
            remote(src, dst, n + j, l_kind + 2 * (to - 1) + j, device)
            for j, (src, dst) in enumerate(((lists_hbm, lists[to]), (lens_hbm, lens[to])))
        ]

    def place(c):
        if c == 0:
            y = jnp.zeros((local * block, inner), jnp.float32)
            for n, part in enumerate(parts):
                loads[n].wait()
                key_loads[n].wait()
                y += jnp.dot(x[:, part], w[c, part], preferred_element_type=jnp.float32)
        else:
            w_loads[c - 1].wait()
            y = jnp.dot(x[...], w[c], preferred_element_type=jnp.float32)
        y = y.astype(jnp.bfloat16)
        for b in range(local):
            rows = y[b * block : (b + 1) * block]
            own = jnp.where(half == 0, rows[:, :per], rows[:, per:])
            across[c, b] = jnp.where(half == 0, rows[:, per:], rows[:, :per])
            if c < 2:
                bufs[c][(view * halves + half) * local + b] = own
            else:
                queries[0, b] = own

    for c in range(3):
        place(c)
        if c == 0:
            pl.semaphore_wait(barrier, jnp.where(at_end, 2, 4))

        @pl.when(at_end)
        def _():
            to_row(c).start()
            to_other(c, diagonal, 2).start()

        @pl.when(jnp.logical_not(at_end))
        def _():
            if c < 1:
                onward(c, -1).start()
            to_other(c, beside, 0).start()
            if c == 1:
                onward(c, -1).start()

    def assemble(own, rest):
        for b in range(local):
            rows = pl.ds(b * block, block)
            out_ref[rows, :per] = jnp.where(half == 0, own[b], rest[b])
            out_ref[rows, per:] = jnp.where(half == 0, rest[b], own[b])

    head_of = lax.broadcasted_iota(jnp.int32, (block, per), 1) // head_size
    heads = [head_of == h for h in range(shared)]

    def weigh(g, i):
        q = queries[g, i]
        stacked = jnp.concatenate([jnp.where(m, q, jnp.zeros_like(q)) for m in heads], axis=0)
        keys = jnp.concatenate([kbuf[lists[g][i, s]] for s in range(slots)], axis=0)
        scores = lax.dot_general(
            stacked, keys, (((1,), (1,)), ((), ())), preferred_element_type=jnp.float32
        ) * head_size ** (-0.5)
        live = lax.broadcasted_iota(jnp.int32, scores.shape, 1) // block < lens[g][i]
        top = jnp.max(jnp.where(live, scores, NEG), axis=1, keepdims=True)
        weights = jnp.where(live, jnp.exp(scores - top), 0.0)
        total_buf[g * local + i] = jnp.sum(weights, axis=1, keepdims=True)
        weight_buf[g * local + i] = weights.astype(jnp.bfloat16)

    def finish(g, i):
        values = jnp.concatenate([vbuf[lists[g][i, s]] for s in range(slots)], axis=0)
        summed = jnp.dot(weight_buf[g * local + i], values, preferred_element_type=jnp.float32)
        scaled = summed / total_buf[g * local + i]
        attn = scaled[:block]
        for h in range(1, shared):
            attn = jnp.where(heads[h], scaled[h * block : (h + 1) * block], attn)
        results[g, i] = attn.astype(jnp.bfloat16)

    def returned(g, i):
        place, device = ((1, beside), (0, mate), (1, diagonal))[g - 1]
        kind = l_kind + 6 + place * local + i
        return remote(results.at[g, i], got.at[place, i], 13 + (g - 1) * local + i, kind, device)

    for load in own_lists:
        load.wait()

    @pl.when(jnp.logical_not(at_end))
    def _():
        for send in list_copies(1, 9, beside):
            send.start()
        for c, n in ((0, 0), (0, 1), (0, 2), (1, 0), (1, 1), (1, 2)):
            arrived(c, n)
            onward(c, n).start()
        for n in range(3):
            remote(across.at[2], queries.at[n + 1], 0, q_kind + n, mate).wait_recv()
        for to in (1, 2, 3):
            for send in list_copies(to, 9, mate):
                send.wait_recv()
        for n in range(3, kinds):
            arrived(0, n)
        for g in (3, 2, 1, 0):
            for i in range(local):
                weigh(g, i)
        for n in range(3, kinds):
            arrived(1, n)
        for first, order in ((0, (2, 3)), (1, (3, 2))):

            @pl.when(half == first)
            def _():
                for g in order:
                    for i in range(local):
                        finish(g, i)
                        returned(g, i).start()

        for g in (1, 0):
            for i in range(local):
                finish(g, i)
                if g:
                    returned(g, i).start()
        for i in range(local):
            returned(1, i).wait_recv()
        assemble(results.at[0], got.at[1])
        for c in range(2):
            for n in range(-1, 3):
                onward(c, n).wait_send()
        for c in range(3):
            to_other(c, beside, 0).wait_send()
        for g in (1, 2, 3):
            for i in range(local):
                returned(g, i).wait_send()
        for send in list_copies(1, 9, beside):
            send.wait_send()

    @pl.when(at_end)
    def _():
        routes = (list_copies(2, 9, mate), list_copies(3, 11, diagonal))
        for route in routes:
            for send in route:
                send.start()
        for g in (2, 3):
            for i in range(local):
                returned(g, i).wait_recv()
        assemble(got.at[0], got.at[1])
        for c in range(3):
            to_row(c).wait_send()
            to_other(c, diagonal, 2).wait_send()
        for route in routes:
            for send in route:
                send.wait_send()


def headwise(sizes, block, tokens, w_qkv, lists, lens, inner):
    views, halves = sizes
    rows, width = tokens.shape
    local, slots = lists.shape
    count, per = views * halves * local, inner // halves
    stacked = HEADS // halves * block
    anywhere = pl.BlockSpec(memory_space=pl.ANY)
    return pl.pallas_call(
        functools.partial(headwise_body, sizes),
        out_shape=pltpu.VMEM((rows, inner), jnp.bfloat16),
        in_specs=[anywhere] * 4,
        out_specs=pl.BlockSpec(memory_space=pltpu.VMEM),
        scratch_shapes=[
            pltpu.VMEM((rows, width), jnp.bfloat16),
            pltpu.VMEM((3, width, inner), jnp.bfloat16),
            pltpu.VMEM((count, block, per), jnp.bfloat16),
            pltpu.VMEM((count, block, per), jnp.bfloat16),
            pltpu.VMEM((3, local, block, per), jnp.bfloat16),
            pltpu.VMEM((4, local, block, per), jnp.bfloat16),
            pltpu.VMEM((4, local, block, per), jnp.bfloat16),
            pltpu.VMEM((2, local, block, per), jnp.bfloat16),
            pltpu.VMEM((4 * local, stacked, slots * block), jnp.bfloat16),
            pltpu.VMEM((4 * local, stacked, 1), jnp.float32),
            pltpu.SemaphoreType.DMA((STEPS,)),
            pltpu.SemaphoreType.DMA((2 + STEPS,)),
            pltpu.SemaphoreType.DMA((2,)),
            pltpu.SemaphoreType.DMA((13 + 3 * local,)),
            pltpu.SemaphoreType.DMA((2, 4)),
            pltpu.SemaphoreType.DMA((24 + 2 * local,)),
            *[pltpu.SMEM((local, slots), jnp.int32)] * 4,
            *[pltpu.SMEM((local,), jnp.int32)] * 4,
        ],
        compiler_params=pltpu.CompilerParams(
            collective_id=0, has_side_effects=True, vmem_limit_bytes=62000000
        ),
    )(lists, lens, tokens, w_qkv)


def mix_body(attn_ref, w_ref, out_ref, buf, sem):
    width = out_ref.shape[1]
    step = width // 4
    copies = []
    for n in range(4):
        cols = pl.ds(n * step, step)
        buf[n] = jnp.dot(
            attn_ref[...], w_ref[:, cols], preferred_element_type=jnp.float32
        ).astype(jnp.bfloat16)
        copies.append(pltpu.make_async_copy(buf.at[n], out_ref.at[:, cols], sem.at[n]))
        copies[-1].start()
    for copy in copies:
        copy.wait()


def project_out(attn, w_out):
    rows, width = attn.shape[0], w_out.shape[1]
    mixed = pl.pallas_call(
        mix_body,
        out_shape=jax.ShapeDtypeStruct((rows, width), jnp.bfloat16),
        in_specs=[pl.BlockSpec(memory_space=pltpu.VMEM), pl.BlockSpec(memory_space=pltpu.VMEM)],
        out_specs=pl.BlockSpec(memory_space=pl.ANY),
        scratch_shapes=[pltpu.VMEM((4, rows, width // 4), jnp.bfloat16), pltpu.SemaphoreType.DMA((4,))],
        compiler_params=pltpu.CompilerParams(vmem_limit_bytes=16000000),
    )(attn, w_out)
    return mixed.reshape(1, rows, width)


def per_device(sizes, tokens, w_qkv, w_out, key_lists, list_len):
    views, halves = sizes
    rows, width = tokens.shape[1:]
    inner = w_out.shape[0]
    local = key_lists.shape[1]
    slots = key_lists.shape[2]
    block = rows // local
    shards = views * halves
    if views == 4 and halves == 2:
        attn = headwise(
            sizes,
            block,
            tokens.reshape(rows, width),
            w_qkv,
            key_lists.reshape(local, slots),
            list_len.reshape(local),
            inner,
        )
        return project_out(attn, w_out)
    anywhere = pl.BlockSpec(memory_space=pl.ANY)
    attn = pl.pallas_call(
        functools.partial(body, sizes),
        out_shape=pltpu.VMEM((rows, inner), jnp.bfloat16),
        in_specs=[
            anywhere,
            anywhere,
            anywhere,
            anywhere,
        ],
        out_specs=pl.BlockSpec(memory_space=pltpu.VMEM),
        scratch_shapes=[
            pltpu.VMEM((rows, width), jnp.bfloat16),
            pltpu.VMEM((3, width, inner), jnp.bfloat16),
            pltpu.VMEM((shards * local, block, inner), jnp.bfloat16),
            pltpu.VMEM((shards * local, block, inner), jnp.bfloat16),
            pltpu.VMEM((local, HEADS * block, slots * block), jnp.bfloat16),
            pltpu.VMEM((local, HEADS * block, 1), jnp.float32),
            pltpu.SemaphoreType.DMA((4,)),
            pltpu.SemaphoreType.DMA((4, 2, shards * local)),
            pltpu.SemaphoreType.DMA((2, shards * local)),
            pltpu.SMEM((local, slots), jnp.int32),
            pltpu.SMEM((local,), jnp.int32),
            pltpu.SemaphoreType.DMA((2,)),
            pltpu.SemaphoreType.DMA((local,)),
        ],
        compiler_params=pltpu.CompilerParams(collective_id=0, has_side_effects=True, vmem_limit_bytes=62000000),
    )(
        key_lists.reshape(local, slots),
        list_len.reshape(local),
        tokens.reshape(rows, width),
        w_qkv,
    )
    return project_out(attn, w_out)


def solution(mesh):
    sizes = (mesh.shape["view"], mesh.shape["half"])
    placed = (
        P(("scene", "view"), "half", None),
        P(),
        P(),
        P(("scene", "view"), "half", None),
        P(("scene", "view"), "half"),
    )
    return jax.shard_map(
        functools.partial(per_device, sizes),
        mesh=mesh,
        in_specs=placed,
        out_specs=P(("scene", "view"), "half", None),
        check_vma=False,
    )
```
